32 devices in a mesh: groups: 2 (over y), path: 4 (over z), half: 2 (over x), tile: 2 (over core).
Axes of the slice: x: 2, y: 2, z: 4, core: 2. Of those that a mesh axis runs over, the one named last changes fastest.
Arguments:
- left_prefix: bfloat16 [64, 4096], P(('groups', 'path'), ('half', 'tile')), parts along dimension 0, may hold values from -6 to 6
- right_prefix: bfloat16 [64, 4096], P(('groups', 'half', 'tile'), 'path'), parts along dimension 0, may hold values from -6 to 6
- left_layer: bfloat16 [2048, 1024], P(('groups', 'half', 'tile')), parts along dimension 0, may hold values from -0.1875 to 0.1875
- right_layer: bfloat16 [2048, 1024], P(('groups', 'path')), parts along dimension 0, may hold values from -0.1875 to 0.1875
- left_map: int32 [512], P('groups'), parts along dimension 0, may hold values from 0 to 31
- right_map: int32 [512], P('groups'), parts along dimension 0, may hold values from 0 to 31
- branch_bits: int32 [512, 10], P('groups'), parts along dimension 0, may hold values 0 or 1
- cut_side: int32 [20], P('groups'), parts along dimension 0, may hold values 0 or 1
Outputs:
- amplitude: bfloat16 [8192, 4096], P(('groups', 'half', 'tile'), 'path'), parts along dimension 0
The draws below stay inside these ranges and needn't reach their ends.
There are 2 independent parts, one for each index of `groups`. The reference program is written for one: setup_inputs(seed, part) draws one part's arguments, and reference() takes and returns one part's arrays. A program takes and returns all parts, laid end to end along the dimension named above; each array names one. Nothing has to cross between parts.
All inputs are finite; a program needn't handle non-finite values.
Results may differ from the reference program's by a relative error of at most 0.0058.
Values may be sent and summed in bfloat16 or wider, within the bound.
A program may use at most 64 MiB of HBM per device.

```python
import jax
import jax.numpy as jnp
from jax import lax

CUTS = 10
GATE = 1024
OUT = 4096
PATHS = 256
PREFIX = 32


def with_ends(drawn, rng, low, high):
    place = [jax.random.randint(jax.random.fold_in(rng, axis), (), 0, length) for axis, length in enumerate(drawn.shape)]
    widest = drawn.shape.index(max(drawn.shape))
    neighbour = place[:widest] + [(place[widest] + 1) % drawn.shape[widest]] + place[widest + 1:]
    return drawn.at[tuple(place)].set(low).at[tuple(neighbour)].set(high)


def level_of(key, extent, split, smallest, high):
    factor_of = 1.0
    for dim, shards_of in split:
        draws = jax.random.uniform(jax.random.fold_in(jax.random.fold_in(key, 6), dim), (shards_of,), jnp.float32, smallest / len(split), high / len(split))
        factor_of = factor_of * jnp.repeat(jnp.exp(draws), extent[dim] // shards_of).reshape((-1,) + (1,) * (len(extent) - 1 - dim))
    return factor_of


def centred(key, dims, deviation, reach, split=(), held_as=jnp.bfloat16):
    drawn = deviation * jax.random.normal(key, dims, jnp.float32)
    if split:
        drawn = drawn * level_of(key, dims, split, -0.22, 0.18)
    return jnp.clip(drawn, -reach, reach).astype(held_as)


def setup_inputs(seed: int = 0, part: int = 0) -> dict:
    key_of = jax.random.split(jax.random.key(seed), 9)
    own_keys = jax.random.split(jax.random.fold_in(key_of[8], part), 9)
    return {
        "left_prefix": centred(own_keys[0], (PREFIX, OUT), 1.0, 6.0, ((0, 4), (1, 4))),
        "right_prefix": centred(own_keys[1], (PREFIX, OUT), 1.0, 6.0, ((0, 4), (1, 4))),
        "left_layer": centred(own_keys[2], (GATE, GATE), GATE ** -0.5, 0.1875, ((0, 4),)),
        "right_layer": centred(own_keys[3], (GATE, GATE), GATE ** -0.5, 0.1875, ((0, 4),)),
        "left_map": with_ends(jax.random.randint(own_keys[4], (PATHS,), 0, PREFIX), jax.random.fold_in(own_keys[4], 1), 0, PREFIX - 1).astype(jnp.int32),
        "right_map": with_ends(jax.random.randint(own_keys[5], (PATHS,), 0, PREFIX), jax.random.fold_in(own_keys[5], 1), 0, PREFIX - 1).astype(jnp.int32),
        "branch_bits": with_ends((jax.random.randint(own_keys[6], (PATHS, CUTS), 0, 2) < 1).astype(jnp.int32), jax.random.fold_in(own_keys[6], 1), 0, 1),
        "cut_side": with_ends((jax.random.randint(own_keys[7], (CUTS,), 0, 2) < 1).astype(jnp.int32), jax.random.fold_in(own_keys[7], 1), 0, 1),
    }


def cut_factors(branch, cut_side, gate_count, on_left):
    cut_count = cut_side.shape[0]
    bit_place = lax.broadcasted_iota(jnp.int32, (cut_count, gate_count), 0)
    gate_code = lax.broadcasted_iota(jnp.int32, (cut_count, gate_count), 1)
    bit_table = jnp.right_shift(gate_code, bit_place) & 1
    projector = cut_side if on_left else 1 - cut_side
    phased = 1 - projector
    chosen = branch * projector[None, :]
    misses = jnp.sum(chosen, axis=1, keepdims=True) + jnp.dot(projector, bit_table)[None, :] - 2 * jnp.dot(chosen, bit_table)
    parity = jnp.dot(branch * phased[None, :], bit_table)
    sign_value = 1 - 2 * (parity % 2)
    return jnp.where(misses == 0, sign_value, 0).astype(jnp.float32)


def half_states(prefix, path_map, branch, cut_side, layer_matrix, on_left):
    gate_count = layer_matrix.shape[0]
    blocks = prefix.shape[1] // gate_count
    count = path_map.shape[0]
    picked = prefix[path_map].reshape(count, blocks, gate_count)
    factor = cut_factors(branch, cut_side, gate_count, on_left)
    projected = (picked.astype(jnp.float32) * factor[:, None, :]).astype(jnp.bfloat16)
    states = jnp.dot(projected.reshape(count * blocks, gate_count), layer_matrix.T, preferred_element_type=jnp.float32)
    return states.astype(jnp.bfloat16).reshape(count, blocks * gate_count)


def reference(left_prefix, right_prefix, left_layer, right_layer, left_map, right_map, branch_bits, cut_side):
    left_states = half_states(left_prefix, left_map, branch_bits, cut_side, left_layer, True)
    right_states = half_states(right_prefix, right_map, branch_bits, cut_side, right_layer, False)
    amplitude = lax.dot_general(left_states, right_states, (((0,), (0,)), ((), ())), preferred_element_type=jnp.float32)
    return amplitude.astype(jnp.bfloat16)
```

```python
import functools

import jax
import jax.numpy as jnp
from jax import lax
from jax.experimental import pallas as pl
from jax.experimental.pallas import tpu as pltpu
from jax.sharding import PartitionSpec as P

MESH = pl.DeviceIdType.MESH
NT = (((1,), (1,)), ((), ()))
TN = (((0,), (0,)), ((), ()))
FULL_MISS = 64.0


def sent_rows(block):
    return max(16, block * 7 // 16 // 16 * 16)


def spread_sides(side_row):
    cuts = side_row.shape[1]
    across = lax.broadcasted_iota(jnp.int32, (cuts, cuts), 0)
    down = lax.broadcasted_iota(jnp.int32, (cuts, cuts), 1)
    return jnp.sum(jnp.where(across == down, side_row, 0.0), axis=1, keepdims=True)


def write_factor(dst, branch, projector):
    cuts, gate = branch.shape[0], dst.shape[1]
    chosen = branch * projector
    table = jnp.concatenate(
        [FULL_MISS * chosen, FULL_MISS * (projector - chosen) + (branch - chosen)], axis=0
    ).astype(jnp.bfloat16)
    width = min(256, gate)
    for at in range(0, gate, width):
        place = lax.broadcasted_iota(jnp.int32, (cuts, width), 0)
        code = lax.broadcasted_iota(jnp.int32, (cuts, width), 1) + at
        bits = (jnp.right_shift(code, place) & 1).astype(jnp.float32)
        both = jnp.concatenate([1.0 - bits, bits], axis=0).astype(jnp.bfloat16)
        count = lax.dot_general(
            table, both, TN, preferred_element_type=jnp.float32
        ).astype(jnp.int32)
        sign = (1 - 2 * (count & 1)).astype(jnp.float32)
        dst[:, at:at + width] = jnp.where(count < int(FULL_MISS), sign, 0.0).astype(jnp.bfloat16)


def one_hot(rows, path_map):
    which = lax.broadcasted_iota(jnp.int32, (rows, path_map.shape[1]), 0)
    return jnp.where(which == path_map, 1.0, 0.0).T.astype(jnp.bfloat16)


def project(dst, hot, prefix, factor):
    gate = prefix.shape[-1]
    rows = prefix.astype(jnp.float32).reshape(-1, gate).astype(jnp.bfloat16)
    picks = hot[...]
    width = min(256, gate)
    for at in range(0, gate, width):
        chosen = jnp.dot(picks, rows[:, at:at + width], preferred_element_type=jnp.float32)
        dst[:, at:at + width] = chosen.astype(jnp.bfloat16) * factor[:, at:at + width]


def nt(a, b):
    return lax.dot_general(a, b, NT, preferred_element_type=jnp.float32).astype(jnp.bfloat16)


def kernel(
    sizes,
    left_prefix, right_prefix, left_layer, right_layer, left_map, right_map, branch_bits, cut_side,
    out,
    map_l, map_r, branch_v, side_v,
    left_rows, right_rows, left_factor, right_factor, own_proj, proj, left_w, right_w,
    left_st, right_st, left_stage, right_stage, hot_l, hot_r,
    near_sem, far_sem, small_sem, own_sem,
    o_send, o_recv, lp_send, lp_recv, rg_send, rg_recv, rz_send, rz_recv,
    w_send, w_recv, ws_send, ws_recv, st_send, st_recv, ss_send, ss_recv, ls_send, ls_recv,
):
    n_half, n_path, n_tile = sizes
    x, z, c = lax.axis_index("half"), lax.axis_index("path"), lax.axis_index("tile")
    sib = 1 - c
    n_lr = n_half * n_tile
    mine = x * n_tile + c
    block_l, gate = left_layer.shape
    block_r = right_layer.shape[0]
    sent = sent_rows(block_l)
    kept = block_l - sent
    chip_l = n_tile * block_l
    hub = lax.rem(z, n_tile)
    is_hub = c == hub
    per_core = n_path // n_tile

    barrier = pltpu.get_barrier_semaphore()

    def loop(n, do):
        if n == 1:
            do(0)
        elif n > 1:
            lax.fori_loop(0, n, lambda t, _: (do(t), 0)[1], 0)

    def remote(src, dst, send, recv, device):
        return pltpu.make_async_remote_copy(
            src_ref=src, dst_ref=dst, send_sem=send, recv_sem=recv, device_id=device, device_id_type=MESH
        )

    def at_l(owner, start, rows):
        return pl.ds(pl.multiple_of(owner * block_l + start, 16), rows)

    def at_r(block):
        return pl.ds(pl.multiple_of(block * block_r, 16), block_r)

    def greet_far(t):
        there = lax.rem(z + 1 + t // n_half, n_path)
        pl.semaphore_signal(
            barrier, inc=1, device_id={"path": there, "half": lax.rem(t, n_half), "tile": 1},
            device_id_type=MESH,
        )

    loop((n_path - 1) * n_half, greet_far)
    for k in range(n_half):
        def greet_near():
            pl.semaphore_signal(
                barrier, inc=1, device_id={"half": lax.rem(x + k, n_half), "tile": 0}, device_id_type=MESH
            )
        if k == 0:
            pl.when(c != 0)(greet_near)
        else:
            greet_near()

    small = [
        pltpu.make_async_copy(src, dst, small_sem.at[i])
        for i, (src, dst) in enumerate(
            ((left_map, map_l), (right_map, map_r), (branch_bits, branch_v), (cut_side, side_v))
        )
    ]
    own = [
        pltpu.make_async_copy(left_prefix, left_rows.at[x, z], own_sem.at[0]),
        pltpu.make_async_copy(left_layer, left_w.at[at_l(mine, 0, block_l)], own_sem.at[1]),
        pltpu.make_async_copy(right_layer, right_w, own_sem.at[2]),
    ]
    own_right = pltpu.make_async_copy(right_prefix, right_rows.at[z, mine], own_sem.at[3])
    for copy in small:
        copy.start()
    pl.when(is_hub)(own_right.start)
    for copy in own:
        copy.start()

    def prepare():
        for copy in small:
            copy.wait()
        side = spread_sides(side_v[...].astype(jnp.float32))
        branch = branch_v[...].astype(jnp.float32)
        write_factor(left_factor, branch, side)
        write_factor(right_factor, branch, 1.0 - side)
        hot_l[...] = one_hot(hot_l.shape[1], map_l[...])
        hot_r[...] = one_hot(hot_r.shape[1], map_r[...])

    def gather_out(to_x):
        return remote(
            right_prefix, right_rows.at[z, mine], rg_send.at[to_x], rg_recv.at[mine],
            {"half": to_x, "tile": hub},
        )

    def gather_in(owner):
        held = right_rows.at[z, owner]
        return remote(held, held, rg_send.at[0], rg_recv.at[owner], {"tile": sib})

    def weights_out(k):
        return remote(
            left_layer.at[pl.ds(0, sent)], left_w.at[at_l(mine, 0, sent)],
            w_send.at[k], w_recv.at[k], {"half": lax.rem(x + k + 1, n_half)},
        )

    def weights_from(k):
        return lax.rem(x + n_half - k - 1, n_half)

    def weights_in(k):
        held = left_w.at[at_l(weights_from(k) * n_tile + c, 0, sent)]
        return remote(held, held, w_send.at[k], w_recv.at[k], {"tile": sib})

    def weights_share(k, core):
        held = left_w.at[at_l(weights_from(k) * n_tile + core, 0, sent)]
        return remote(held, held, ws_send.at[k], ws_recv.at[k], {"tile": sib})

    def layer_share(core):
        return remote(
            left_layer, left_w.at[at_l(x * n_tile + core, 0, block_l)], o_send.at[0], o_recv.at[0], {"tile": sib}
        )

    def left_out(to_x, to_z):
        return remote(
            left_prefix, left_rows.at[x, z], lp_send.at[to_x, to_z], lp_recv.at[x, z],
            {"half": to_x, "path": to_z},
        )

    def left_in(from_x, from_z):
        held = left_rows.at[from_x, from_z]
        return remote(held, held, lp_send.at[from_x, from_z], lp_recv.at[from_x, from_z], {"tile": sib})

    def blocks_out(to_z):
        return remote(right_rows.at[z], right_rows.at[z], rz_send.at[to_z], rz_recv.at[z], {"path": to_z})

    def blocks_in(block):
        held = right_rows.at[block]
        return remote(held, held, rz_send.at[block], rz_recv.at[block], {"path": block})

    def states_out(block):
        return remote(
            right_stage.at[block // n_tile], right_st.at[at_r(z)], st_send.at[block], st_recv.at[z], {"path": block}
        )

    def states_in(block):
        held = right_st.at[at_r(block)]
        return remote(held, held, st_send.at[block], st_recv.at[block], {"path": block})

    def states_share(block):
        held = right_st.at[at_r(block)]
        return remote(held, held, ss_send.at[block], ss_recv.at[block], {"tile": sib})

    def left_states_out(k, core):
        to_x = lax.rem(x + k + 1, n_half)
        return remote(
            left_stage.at[k, core], left_st.at[at_l(x * n_tile + core, sent, kept)],
            ls_send.at[k, core], ls_recv.at[k, core], {"half": to_x},
        )

    def left_states_in(k, core):
        held = left_st.at[at_l(weights_from(k) * n_tile + core, sent, kept)]
        return remote(held, held, ls_send.at[k, core], ls_recv.at[k, core], {"tile": sib})

    def others(n, me, do):
        def step(t):
            pl.when(t != me)(lambda: do(t))
        loop(n, step)

    early = z * 2 < n_path
    @pl.when(c == 0)
    def _():
        pl.semaphore_wait(barrier, n_lr - 1)
        pl.semaphore_signal(near_sem, inc=1, device_id={"tile": sib}, device_id_type=MESH)
    @pl.when(c != 0)
    def _():
        pl.semaphore_wait(near_sem, 1)

    for k in range(n_half):
        to_x = lax.rem(x + k, n_half)
        if k == 0:
            pl.when(jnp.logical_not(is_hub))(gather_out(to_x).start)
        else:
            gather_out(to_x).start()
            left_out(to_x, z).start()
    for k in range(n_half - 1):
        weights_out(k).start()
    layer_share(c).start()
    pl.when(early)(prepare)

    if n_path > 1:
        @pl.when(c != 0)
        def _():
            pl.semaphore_wait(barrier, (n_path - 1) * n_lr)
            pl.semaphore_signal(far_sem, inc=1, device_id={"tile": sib}, device_id_type=MESH)
        @pl.when(c == 0)
        def _():
            pl.semaphore_wait(far_sem, 1)

    def prefix_to(to_z):
        for k in range(n_half):
            left_out(lax.rem(x + n_half - 1 - k, n_half), to_z).start()
    others(n_path, z, prefix_to)

    @pl.when(is_hub)
    def _():
        own_right.wait()
        others(n_lr, mine, lambda owner: gather_in(owner).wait_recv())
        others(n_path, z, lambda k: blocks_out(k).start())
    pl.when(jnp.logical_not(early))(prepare)

    own[0].wait()
    own[1].wait()
    layer_share(sib).wait_recv()
    def form_left(k):
        to_x = lax.rem(x + k + 1, n_half)
        loop(n_path, lambda t: left_in(to_x, t).wait_recv())
        project(proj, hot_l, left_rows[to_x], left_factor)
        for core in range(n_tile):
            left_stage[k, core] = nt(left_w[at_l(x * n_tile + core, sent, kept), :], proj[...])
            left_states_out(k, core).start()
    loop(n_half - 1, form_left)

    own[2].wait()
    first = jnp.where(is_hub, z // n_tile + 1, 0)
    def form_right(j):
        block = lax.rem(first + j, per_core) * n_tile + c
        @pl.when(block != z)
        def _():
            blocks_in(block).wait_recv()
        project(proj, hot_r, right_rows[block], right_factor)
        states = nt(right_w[...], proj[...])
        @pl.when(block != z)
        def _():
            right_stage[block // n_tile] = states
            states_out(block).start()
        @pl.when(block == z)
        def _():
            right_st[at_r(z), :] = states
            states_share(z).start()
    loop(per_core, form_right)

    others(n_path, z, lambda t: left_in(x, t).wait_recv())
    project(own_proj, hot_l, left_rows[x], left_factor)
    for core in range(n_tile):
        span = at_l(x * n_tile + core, 0, block_l)
        left_st[span, :] = nt(left_w[span, :], own_proj[...])

    def take_weights(k):
        weights_in(k).wait_recv()
        weights_share(k, c).start()
        span = at_l(weights_from(k) * n_tile + c, 0, sent)
        left_st[span, :] = nt(left_w[span, :], own_proj[...])
    loop(n_half - 1, take_weights)
    def take_shared(k):
        weights_share(k, sib).wait_recv()
        span = at_l(weights_from(k) * n_tile + sib, 0, sent)
        left_st[span, :] = nt(left_w[span, :], own_proj[...])
    loop(n_half - 1, take_shared)

    unit = max(block_r, 128)
    in_unit = unit // block_r
    n_units = n_path // in_unit

    def amplitude(rows, cols):
        out[rows, cols] = nt(left_st[rows, :], right_st[cols, :])

    def right_ready(block):
        @pl.when(is_hub)
        def _():
            @pl.when(block != z)
            def _():
                states_in(block).wait_recv()
                states_share(block).start()
        @pl.when(jnp.logical_not(is_hub))
        def _():
            states_share(block).wait_recv()

    def take_right(u):
        at = lax.rem(z // in_unit + u, n_units)
        for i in range(in_unit):
            right_ready(at * in_unit + i)
        cols = pl.ds(pl.multiple_of(at * unit, 128), unit)
        amplitude(pl.ds(pl.multiple_of(x * chip_l, 16), chip_l), cols)
        def come(k):
            for core in range(n_tile):
                amplitude(at_l(weights_from(k) * n_tile + core, 0, sent), cols)
        loop(n_half - 1, come)
    loop(n_units, take_right)

    def take_left(k):
        for core in range(n_tile):
            left_states_in(k, core).wait_recv()
            amplitude(at_l(weights_from(k) * n_tile + core, sent, kept), slice(None))
    loop(n_half - 1, take_left)

    def left_gone(to_z):
        def to(to_x):
            @pl.when(jnp.logical_or(to_x != x, to_z != z))
            def _():
                left_out(to_x, to_z).wait_send()
        loop(n_half, to)
    loop(n_path, left_gone)
    def gather_gone(to_x):
        @pl.when(jnp.logical_or(to_x != x, jnp.logical_not(is_hub)))
        def _():
            gather_out(to_x).wait_send()
    loop(n_half, gather_gone)
    layer_share(c).wait_send()
    def x_gone(k):
        weights_out(k).wait_send()
        weights_share(k, c).wait_send()
        for core in range(n_tile):
            left_states_out(k, core).wait_send()
    loop(n_half - 1, x_gone)
    def right_gone(j):
        block = j * n_tile + c
        @pl.when(block != z)
        def _():
            states_out(block).wait_send()
    loop(per_core, right_gone)
    @pl.when(is_hub)
    def _():
        loop(n_path, lambda block: states_share(block).wait_send())
        others(n_path, z, lambda to_z: blocks_out(to_z).wait_send())


def on_device(
    sizes,
    left_prefix, right_prefix, left_layer, right_layer, left_map, right_map, branch_bits, cut_side,
):
    n_half, n_path, n_tile = sizes
    n_lr = n_half * n_tile
    paths = left_map.shape[0]
    cuts = cut_side.shape[0]
    block_l, gate = left_layer.shape
    block_r = right_layer.shape[0]
    rows_l, rows_r = block_l * n_lr, block_r * n_path
    kept = block_l - sent_rows(block_l)
    many = max(1, n_half - 1)
    dma = pltpu.SemaphoreType.DMA
    bf16, i32 = jnp.bfloat16, jnp.int32
    hbm = pl.BlockSpec(memory_space=pltpu.HBM)
    return pl.pallas_call(
        functools.partial(kernel, sizes),
        out_shape=jax.ShapeDtypeStruct((rows_l, rows_r), bf16),
        in_specs=[hbm] * 8,
        out_specs=pl.BlockSpec(memory_space=pltpu.VMEM),
        scratch_shapes=[
            pltpu.VMEM((1, paths), i32), pltpu.VMEM((1, paths), i32),
            pltpu.VMEM((cuts, paths), i32), pltpu.VMEM((1, cuts), i32),
            pltpu.VMEM((n_half, n_path) + left_prefix.shape, bf16),
            pltpu.VMEM((n_path, n_lr) + right_prefix.shape, bf16),
            pltpu.VMEM((paths, gate), bf16), pltpu.VMEM((paths, gate), bf16),
            pltpu.VMEM((paths, gate), bf16), pltpu.VMEM((paths, gate), bf16),
            pltpu.VMEM((rows_l, gate), bf16), pltpu.VMEM((block_r, gate), bf16),
            pltpu.VMEM((rows_l, paths), bf16), pltpu.VMEM((rows_r, paths), bf16),
            pltpu.VMEM((many, n_tile, kept, paths), bf16),
            pltpu.VMEM((n_path // n_tile, block_r, paths), bf16),
            pltpu.VMEM((paths, left_prefix.shape[0] * n_path), bf16),
            pltpu.VMEM((paths, right_prefix.shape[0] * n_lr), bf16),
            pltpu.SemaphoreType.REGULAR, pltpu.SemaphoreType.REGULAR, dma((4,)), dma((4,)),
            dma((1,)), dma((1,)), dma((n_half, n_path)), dma((n_half, n_path)),
            dma((n_half,)), dma((n_lr,)), dma((n_path,)), dma((n_path,)),
            dma((many,)), dma((many,)), dma((many,)), dma((many,)),
            dma((n_path,)), dma((n_path,)), dma((n_path,)), dma((n_path,)),
            dma((many, n_tile)), dma((many, n_tile)),
        ],
        compiler_params=pltpu.CompilerParams(
            collective_id=0, has_side_effects=True, vmem_limit_bytes=40 * 2**20
        ),
    )(
        left_prefix, right_prefix, left_layer, right_layer,
        left_map[None, :], right_map[None, :], branch_bits.T, cut_side[None, :],
    )


def solution(mesh):
    in_specs = (
        P(("groups", "path"), ("half", "tile")),
        P(("groups", "half", "tile"), "path"),
        P(("groups", "half", "tile"), None),
        P(("groups", "path"), None),
        P("groups"),
        P("groups"),
        P("groups", None),
        P("groups"),
    )
    out_specs = P(("groups", "half", "tile"), "path")
    sizes = tuple(mesh.shape[axis] for axis in ("half", "path", "tile"))
    return jax.shard_map(
        functools.partial(on_device, sizes),
        mesh=mesh, in_specs=in_specs, out_specs=out_specs, check_vma=False,
    )
```

```python
import functools

import jax
import jax.numpy as jnp
from jax import lax
from jax.experimental import pallas as pl
from jax.experimental.pallas import tpu as pltpu
from jax.sharding import PartitionSpec as P

MESH = pl.DeviceIdType.MESH
NT = (((1,), (1,)), ((), ()))
TN = (((0,), (0,)), ((), ()))
FULL_MISS = 64.0


def sent_rows(block):
    return max(16, block * 7 // 16 // 16 * 16)


def spread_sides(side_row):
    cuts = side_row.shape[1]
    across = lax.broadcasted_iota(jnp.int32, (cuts, cuts), 0)
    down = lax.broadcasted_iota(jnp.int32, (cuts, cuts), 1)
    return jnp.sum(jnp.where(across == down, side_row, 0.0), axis=1, keepdims=True)


def write_factor(dst, branch, projector):
    cuts, gate = branch.shape[0], dst.shape[1]
    chosen = branch * projector
    table = jnp.concatenate(
        [FULL_MISS * chosen, FULL_MISS * (projector - chosen) + (branch - chosen)], axis=0
    ).astype(jnp.bfloat16)
    width = min(256, gate)
    for at in range(0, gate, width):
        place = lax.broadcasted_iota(jnp.int32, (cuts, width), 0)
        code = lax.broadcasted_iota(jnp.int32, (cuts, width), 1) + at
        bits = (jnp.right_shift(code, place) & 1).astype(jnp.float32)
        both = jnp.concatenate([1.0 - bits, bits], axis=0).astype(jnp.bfloat16)
        count = lax.dot_general(
            table, both, TN, preferred_element_type=jnp.float32
        ).astype(jnp.int32)
        sign = (1 - 2 * (count & 1)).astype(jnp.float32)
        dst[:, at:at + width] = jnp.where(count < int(FULL_MISS), sign, 0.0).astype(jnp.bfloat16)


def one_hot(rows, path_map):
    which = lax.broadcasted_iota(jnp.int32, (rows, path_map.shape[1]), 0)
    return jnp.where(which == path_map, 1.0, 0.0).T.astype(jnp.bfloat16)


def project(dst, hot, prefix, factor):
    gate = prefix.shape[-1]
    rows = prefix.astype(jnp.float32).reshape(-1, gate).astype(jnp.bfloat16)
    picks = hot[...]
    width = min(256, gate)
    for at in range(0, gate, width):
        chosen = jnp.dot(picks, rows[:, at:at + width], preferred_element_type=jnp.float32)
        dst[:, at:at + width] = chosen.astype(jnp.bfloat16) * factor[:, at:at + width]


def nt(a, b):
    return lax.dot_general(a, b, NT, preferred_element_type=jnp.float32).astype(jnp.bfloat16)


def kernel(
    sizes,
    left_prefix, right_prefix, left_layer, right_layer, left_map, right_map, branch_bits, cut_side,
    out,
    map_l, map_r, branch_v, side_v,
    left_rows, right_rows, left_factor, right_factor, own_proj, proj, left_w, right_w,
    left_st, right_st, left_stage, right_stage, hot_l, hot_r,
    near_sem, far_sem, small_sem, own_sem,
    o_send, o_recv, lp_send, lp_recv, rg_send, rg_recv, rz_send, rz_recv,
    w_send, w_recv, ws_send, ws_recv, st_send, st_recv, ss_send, ss_recv, ls_send, ls_recv,
):
    n_half, n_path, n_tile = sizes
    x, z, c = lax.axis_index("half"), lax.axis_index("path"), lax.axis_index("tile")
    sib = 1 - c
    n_lr = n_half * n_tile
    mine = x * n_tile + c
    block_l, gate = left_layer.shape
    block_r = right_layer.shape[0]
    sent = sent_rows(block_l)
    kept = block_l - sent
    chip_l = n_tile * block_l
    hub = lax.rem(z, n_tile)
    is_hub = c == hub
    per_core = n_path // n_tile

    barrier = pltpu.get_barrier_semaphore()

    def loop(n, do):
        if n == 1:
            do(0)
        elif n > 1:
            lax.fori_loop(0, n, lambda t, _: (do(t), 0)[1], 0)

    def remote(src, dst, send, recv, device):
        return pltpu.make_async_remote_copy(
            src_ref=src, dst_ref=dst, send_sem=send, recv_sem=recv, device_id=device, device_id_type=MESH
        )

    def at_l(owner, start, rows):
        return pl.ds(pl.multiple_of(owner * block_l + start, 16), rows)

    def at_r(block):
        return pl.ds(pl.multiple_of(block * block_r, 16), block_r)

    def greet_far(t):
        there = lax.rem(z + 1 + t // n_half, n_path)
        pl.semaphore_signal(
            barrier, inc=1, device_id={"path": there, "half": lax.rem(t, n_half), "tile": 1},
            device_id_type=MESH,
        )

    loop((n_path - 1) * n_half, greet_far)
    for k in range(n_half):
        def greet_near():
            pl.semaphore_signal(
                barrier, inc=1, device_id={"half": lax.rem(x + k, n_half), "tile": 0}, device_id_type=MESH
            )
        if k == 0:
            pl.when(c != 0)(greet_near)
        else:
            greet_near()

    small = [
        pltpu.make_async_copy(src, dst, small_sem.at[i])
        for i, (src, dst) in enumerate(
            ((left_map, map_l), (right_map, map_r), (branch_bits, branch_v), (cut_side, side_v))
        )
    ]
    own = [
        pltpu.make_async_copy(left_prefix, left_rows.at[x, z], own_sem.at[0]),
        pltpu.make_async_copy(left_layer, left_w.at[at_l(mine, 0, block_l)], own_sem.at[1]),
        pltpu.make_async_copy(right_layer, right_w, own_sem.at[2]),
    ]
    own_right = pltpu.make_async_copy(right_prefix, right_rows.at[z, mine], own_sem.at[3])
    for copy in small:
        copy.start()
    pl.when(is_hub)(own_right.start)
    for copy in own:
        copy.start()

    def prepare():
        for copy in small:
            copy.wait()
        side = spread_sides(side_v[...].astype(jnp.float32))
        branch = branch_v[...].astype(jnp.float32)
        write_factor(left_factor, branch, side)
        write_factor(right_factor, branch, 1.0 - side)
        hot_l[...] = one_hot(hot_l.shape[1], map_l[...])
        hot_r[...] = one_hot(hot_r.shape[1], map_r[...])

    def gather_out(to_x):
        return remote(
            right_prefix, right_rows.at[z, mine], rg_send.at[to_x], rg_recv.at[mine],
            {"half": to_x, "tile": hub},
        )

    def gather_in(owner):
        held = right_rows.at[z, owner]
        return remote(held, held, rg_send.at[0], rg_recv.at[owner], {"tile": sib})

    def weights_out(k):
        return remote(
            left_layer.at[pl.ds(0, sent)], left_w.at[at_l(mine, 0, sent)],
            w_send.at[k], w_recv.at[k], {"half": lax.rem(x + k + 1, n_half)},
        )

    def weights_from(k):
        return lax.rem(x + n_half - k - 1, n_half)

    def weights_in(k):
        held = left_w.at[at_l(weights_from(k) * n_tile + c, 0, sent)]
        return remote(held, held, w_send.at[k], w_recv.at[k], {"tile": sib})

    def weights_share(k, core):
        held = left_w.at[at_l(weights_from(k) * n_tile + core, 0, sent)]
        return remote(held, held, ws_send.at[k], ws_recv.at[k], {"tile": sib})

    def layer_share(core):
        return remote(
            left_layer, left_w.at[at_l(x * n_tile + core, 0, block_l)], o_send.at[0], o_recv.at[0], {"tile": sib}
        )

    def left_out(to_x, to_z):
        return remote(
            left_prefix, left_rows.at[x, z], lp_send.at[to_x, to_z], lp_recv.at[x, z],
            {"half": to_x, "path": to_z},
        )

    def left_in(from_x, from_z):
        held = left_rows.at[from_x, from_z]
        return remote(held, held, lp_send.at[from_x, from_z], lp_recv.at[from_x, from_z], {"tile": sib})

    def blocks_out(to_z):
        return remote(right_rows.at[z], right_rows.at[z], rz_send.at[to_z], rz_recv.at[z], {"path": to_z})

    def blocks_in(block):
        held = right_rows.at[block]
        return remote(held, held, rz_send.at[block], rz_recv.at[block], {"path": block})

    def states_out(block):
        return remote(
            right_stage.at[block // n_tile], right_st.at[at_r(z)], st_send.at[block], st_recv.at[z], {"path": block}
        )

    def states_in(block):
        held = right_st.at[at_r(block)]
        return remote(held, held, st_send.at[block], st_recv.at[block], {"path": block})

    def states_share(block):
        held = right_st.at[at_r(block)]
        return remote(held, held, ss_send.at[block], ss_recv.at[block], {"tile": sib})

    def left_states_out(k, core):
        to_x = lax.rem(x + k + 1, n_half)
        return remote(
            left_stage.at[k, core], left_st.at[at_l(x * n_tile + core, sent, kept)],
            ls_send.at[k, core], ls_recv.at[k, core], {"half": to_x},
        )

    def left_states_in(k, core):
        held = left_st.at[at_l(weights_from(k) * n_tile + core, sent, kept)]
        return remote(held, held, ls_send.at[k, core], ls_recv.at[k, core], {"tile": sib})

    def others(n, me, do):
        def step(t):
            pl.when(t != me)(lambda: do(t))
        loop(n, step)

    early = z * 2 < n_path
    @pl.when(c == 0)
    def _():
        pl.semaphore_wait(barrier, n_lr - 1)
        pl.semaphore_signal(near_sem, inc=1, device_id={"tile": sib}, device_id_type=MESH)
    @pl.when(c != 0)
    def _():
        pl.semaphore_wait(near_sem, 1)

    for k in range(n_half):
        to_x = lax.rem(x + k, n_half)
        if k == 0:
            pl.when(jnp.logical_not(is_hub))(gather_out(to_x).start)
        else:
            gather_out(to_x).start()
            left_out(to_x, z).start()
    for k in range(n_half - 1):
        weights_out(k).start()
    layer_share(c).start()
    pl.when(early)(prepare)

    if n_path > 1:
        @pl.when(c != 0)
        def _():
            pl.semaphore_wait(barrier, (n_path - 1) * n_lr)
            pl.semaphore_signal(far_sem, inc=1, device_id={"tile": sib}, device_id_type=MESH)
        @pl.when(c == 0)
        def _():
            pl.semaphore_wait(far_sem, 1)

    def prefix_to(to_z):
        for k in range(n_half):
            left_out(lax.rem(x + n_half - 1 - k, n_half), to_z).start()
    others(n_path, z, prefix_to)

    @pl.when(is_hub)
    def _():
        own_right.wait()
        others(n_lr, mine, lambda owner: gather_in(owner).wait_recv())
        others(n_path, z, lambda k: blocks_out(k).start())
    pl.when(jnp.logical_not(early))(prepare)

    own[0].wait()
    own[1].wait()
    layer_share(sib).wait_recv()
    def form_left(k):
        to_x = lax.rem(x + k + 1, n_half)
        loop(n_path, lambda t: left_in(to_x, t).wait_recv())
        project(proj, hot_l, left_rows[to_x], left_factor)
        for core in range(n_tile):
            left_stage[k, core] = nt(left_w[at_l(x * n_tile + core, sent, kept), :], proj[...])
            left_states_out(k, core).start()
    loop(n_half - 1, form_left)

    own[2].wait()
    first = jnp.where(is_hub, z // n_tile + 1, 0)
    def form_right(j):
        block = lax.rem(first + j, per_core) * n_tile + c
        @pl.when(block != z)
        def _():
            blocks_in(block).wait_recv()
        project(proj, hot_r, right_rows[block], right_factor)
        states = nt(right_w[...], proj[...])
        @pl.when(block != z)
        def _():
            right_stage[block // n_tile] = states
            states_out(block).start()
        @pl.when(block == z)
        def _():
            right_st[at_r(z), :] = states
            states_share(z).start()
    loop(per_core, form_right)

    others(n_path, z, lambda t: left_in(x, t).wait_recv())
    project(own_proj, hot_l, left_rows[x], left_factor)
    for core in range(n_tile):
        span = at_l(x * n_tile + core, 0, block_l)
        left_st[span, :] = nt(left_w[span, :], own_proj[...])

    def take_weights(k):
        weights_in(k).wait_recv()
        weights_share(k, c).start()
        span = at_l(weights_from(k) * n_tile + c, 0, sent)
        left_st[span, :] = nt(left_w[span, :], own_proj[...])
    loop(n_half - 1, take_weights)
    def take_shared(k):
        weights_share(k, sib).wait_recv()
        span = at_l(weights_from(k) * n_tile + sib, 0, sent)
        left_st[span, :] = nt(left_w[span, :], own_proj[...])
    loop(n_half - 1, take_shared)

    unit = max(block_r, 128)
    in_unit = unit // block_r
    n_units = n_path // in_unit

    def amplitude(rows, cols):
        out[rows, cols] = nt(left_st[rows, :], right_st[cols, :])

    def right_ready(block):
        @pl.when(is_hub)
        def _():
            @pl.when(block != z)
            def _():
                states_in(block).wait_recv()
                states_share(block).start()
        @pl.when(jnp.logical_not(is_hub))
        def _():
            states_share(block).wait_recv()

    def take_right(u):
        at = lax.rem(z // in_unit + u, n_units)
        for i in range(in_unit):
            right_ready(at * in_unit + i)
        cols = pl.ds(pl.multiple_of(at * unit, 128), unit)
        amplitude(pl.ds(pl.multiple_of(x * chip_l, 16), chip_l), cols)
        def come(k):
            for core in range(n_tile):
                amplitude(at_l(weights_from(k) * n_tile + core, 0, sent), cols)
        loop(n_half - 1, come)
    loop(n_units, take_right)

    def take_left(k):
        for core in range(n_tile):
            left_states_in(k, core).wait_recv()
            amplitude(at_l(weights_from(k) * n_tile + core, sent, kept), slice(None))
    loop(n_half - 1, take_left)

    def left_gone(to_z):
        def to(to_x):
            @pl.when(jnp.logical_or(to_x != x, to_z != z))
            def _():
                left_out(to_x, to_z).wait_send()
        loop(n_half, to)
    loop(n_path, left_gone)
    def gather_gone(to_x):
        @pl.when(jnp.logical_or(to_x != x, jnp.logical_not(is_hub)))
        def _():
            gather_out(to_x).wait_send()
    loop(n_half, gather_gone)
    layer_share(c).wait_send()
    def x_gone(k):
        weights_out(k).wait_send()
        weights_share(k, c).wait_send()
        for core in range(n_tile):
            left_states_out(k, core).wait_send()
    loop(n_half - 1, x_gone)
    def right_gone(j):
        block = j * n_tile + c
        @pl.when(block != z)
        def _():
            states_out(block).wait_send()
    loop(per_core, right_gone)
    @pl.when(is_hub)
    def _():
        loop(n_path, lambda block: states_share(block).wait_send())
        others(n_path, z, lambda to_z: blocks_out(to_z).wait_send())


def on_device(
    sizes,
    left_prefix, right_prefix, left_layer, right_layer, left_map, right_map, branch_bits, cut_side,
):
    n_half, n_path, n_tile = sizes
    n_lr = n_half * n_tile
    paths = left_map.shape[0]
    cuts = cut_side.shape[0]
    block_l, gate = left_layer.shape
    block_r = right_layer.shape[0]
    rows_l, rows_r = block_l * n_lr, block_r * n_path
    kept = block_l - sent_rows(block_l)
    many = max(1, n_half - 1)
    dma = pltpu.SemaphoreType.DMA
    bf16, i32 = jnp.bfloat16, jnp.int32
    hbm = pl.BlockSpec(memory_space=pltpu.HBM)
    return pl.pallas_call(
        functools.partial(kernel, sizes),
        out_shape=jax.ShapeDtypeStruct((rows_l, rows_r), bf16),
        in_specs=[hbm] * 8,
        out_specs=pl.BlockSpec(memory_space=pltpu.VMEM),
        scratch_shapes=[
            pltpu.VMEM((1, paths), i32), pltpu.VMEM((1, paths), i32),
            pltpu.VMEM((cuts, paths), i32), pltpu.VMEM((1, cuts), i32),
            pltpu.VMEM((n_half, n_path) + left_prefix.shape, bf16),
            pltpu.VMEM((n_path, n_lr) + right_prefix.shape, bf16),
            pltpu.VMEM((paths, gate), bf16), pltpu.VMEM((paths, gate), bf16),
            pltpu.VMEM((paths, gate), bf16), pltpu.VMEM((paths, gate), bf16),
            pltpu.VMEM((rows_l, gate), bf16), pltpu.VMEM((block_r, gate), bf16),
            pltpu.VMEM((rows_l, paths), bf16), pltpu.VMEM((rows_r, paths), bf16),
            pltpu.VMEM((many, n_tile, kept, paths), bf16),
            pltpu.VMEM((n_path // n_tile, block_r, paths), bf16),
            pltpu.VMEM((paths, left_prefix.shape[0] * n_path), bf16),
            pltpu.VMEM((paths, right_prefix.shape[0] * n_lr), bf16),
            pltpu.SemaphoreType.REGULAR, pltpu.SemaphoreType.REGULAR, dma((4,)), dma((4,)),
            dma((1,)), dma((1,)), dma((n_half, n_path)), dma((n_half, n_path)),
            dma((n_half,)), dma((n_lr,)), dma((n_path,)), dma((n_path,)),
            dma((many,)), dma((many,)), dma((many,)), dma((many,)),
            dma((n_path,)), dma((n_path,)), dma((n_path,)), dma((n_path,)),
            dma((many, n_tile)), dma((many, n_tile)),
        ],
        compiler_params=pltpu.CompilerParams(
            collective_id=0, has_side_effects=True, vmem_limit_bytes=40 * 2**20
        ),
    )(*(
        pltpu.with_memory_space_constraint(array, pltpu.HBM) for array in (
            left_prefix, right_prefix, left_layer, right_layer,
            left_map[None, :], right_map[None, :], branch_bits.T, cut_side[None, :],
        )
    ))


def solution(mesh):
    in_specs = (
        P(("groups", "path"), ("half", "tile")),
        P(("groups", "half", "tile"), "path"),
        P(("groups", "half", "tile"), None),
        P(("groups", "path"), None),
        P("groups"),
        P("groups"),
        P("groups", None),
        P("groups"),
    )
    out_specs = P(("groups", "half", "tile"), "path")
    sizes = tuple(mesh.shape[axis] for axis in ("half", "path", "tile"))
    return jax.shard_map(
        functools.partial(on_device, sizes),
        mesh=mesh, in_specs=in_specs, out_specs=out_specs, check_vma=False,
    )
```

```python
import functools

import jax
import jax.numpy as jnp
from jax import lax
from jax.experimental import pallas as pl
from jax.experimental.pallas import tpu as pltpu
from jax.sharding import PartitionSpec as P

MESH = pl.DeviceIdType.MESH
NT = (((1,), (1,)), ((), ()))
TN = (((0,), (0,)), ((), ()))
FULL_MISS = 64.0


def sent_rows(block):
    return max(16, block * 7 // 16 // 16 * 16)


def spread_sides(side_row):
    cuts = side_row.shape[1]
    across = lax.broadcasted_iota(jnp.int32, (cuts, cuts), 0)
    down = lax.broadcasted_iota(jnp.int32, (cuts, cuts), 1)
    return jnp.sum(jnp.where(across == down, side_row, 0.0), axis=1, keepdims=True)


def write_factor(dst, branch, projector):
    cuts, gate = branch.shape[0], dst.shape[1]
    chosen = branch * projector
    table = jnp.concatenate(
        [FULL_MISS * chosen, FULL_MISS * (projector - chosen) + (branch - chosen)], axis=0
    ).astype(jnp.bfloat16)
    width = min(256, gate)
    for at in range(0, gate, width):
        place = lax.broadcasted_iota(jnp.int32, (cuts, width), 0)
        code = lax.broadcasted_iota(jnp.int32, (cuts, width), 1) + at
        bits = (jnp.right_shift(code, place) & 1).astype(jnp.float32)
        both = jnp.concatenate([1.0 - bits, bits], axis=0).astype(jnp.bfloat16)
        count = lax.dot_general(
            table, both, TN, preferred_element_type=jnp.float32
        ).astype(jnp.int32)
        sign = (1 - 2 * (count & 1)).astype(jnp.float32)
        dst[:, at:at + width] = jnp.where(count < int(FULL_MISS), sign, 0.0).astype(jnp.bfloat16)


def one_hot(rows, path_map):
    which = lax.broadcasted_iota(jnp.int32, (rows, path_map.shape[1]), 0)
    return jnp.where(which == path_map, 1.0, 0.0).T.astype(jnp.bfloat16)


def project(dst, hot, prefix, factor):
    gate = prefix.shape[-1]
    rows = prefix.astype(jnp.float32).reshape(-1, gate).astype(jnp.bfloat16)
    picks = hot[...]
    width = min(256, gate)
    for at in range(0, gate, width):
        chosen = jnp.dot(picks, rows[:, at:at + width], preferred_element_type=jnp.float32)
        dst[:, at:at + width] = chosen.astype(jnp.bfloat16) * factor[:, at:at + width]


def nt(a, b):
    return lax.dot_general(a, b, NT, preferred_element_type=jnp.float32).astype(jnp.bfloat16)


def kernel(
    sizes,
    left_prefix, right_prefix, left_layer, right_layer, left_map, right_map, branch_bits, cut_side,
    out,
    map_l, map_r, branch_v, side_v,
    left_rows, right_rows, left_factor, right_factor, own_proj, proj, left_w, right_w,
    left_st, right_st, left_stage, right_stage, hot_l, hot_r,
    near_sem, far_sem, small_sem, own_sem,
    o_send, o_recv, lp_send, lp_recv, lx_send, lx_recv, rg_send, rg_recv, rz_send, rz_recv,
    w_send, w_recv, ws_send, ws_recv, st_send, st_recv, ss_send, ss_recv, ls_send, ls_recv,
):
    n_half, n_path, n_tile = sizes
    x, z, c = lax.axis_index("half"), lax.axis_index("path"), lax.axis_index("tile")
    sib = 1 - c
    n_lr = n_half * n_tile
    mine = x * n_tile + c
    block_l, gate = left_layer.shape
    block_r = right_layer.shape[0]
    sent = sent_rows(block_l)
    kept = block_l - sent
    chip_l = n_tile * block_l
    known = chip_l + (n_half - 1) * n_tile * sent
    hub = lax.rem(z, n_tile)
    is_hub = c == hub
    per_core = n_path // n_tile
    early = z * 2 < n_path
    late = jnp.logical_not(early)

    barrier = pltpu.get_barrier_semaphore()

    def loop(n, do):
        if n == 1:
            do(0)
        elif n > 1:
            lax.fori_loop(0, n, lambda t, _: (do(t), 0)[1], 0)

    def others(n, me, do):
        def step(t):
            pl.when(t != me)(lambda: do(t))
        loop(n, step)

    def remote(src, dst, send, recv, device):
        return pltpu.make_async_remote_copy(
            src_ref=src, dst_ref=dst, send_sem=send, recv_sem=recv, device_id=device, device_id_type=MESH
        )

    def signal(sem, device):
        pl.semaphore_signal(sem, inc=1, device_id=device, device_id_type=MESH)

    def span(start, rows):
        return pl.ds(start if isinstance(start, int) else pl.multiple_of(start, 16), rows)

    def own_sent(core):
        return span(core * sent, sent)

    def own_kept(core):
        return span(n_tile * sent + core * kept, kept)

    def other_sent(k, core):
        return span(chip_l + (k * n_tile + core) * sent, sent)

    def other_kept(k):
        return span(known + k * n_tile * kept, n_tile * kept)

    def at_r(block):
        return span(block * block_r, block_r)

    def to_x(k):
        return lax.rem(x + k + 1, n_half)

    def from_x(k):
        return lax.rem(x + n_half - k - 1, n_half)

    def greet_column(t):
        there = lax.rem(z + 1 + t, n_path)
        signal(barrier, {"path": there, "tile": 1})

    loop(n_path - 1, greet_column)
    @pl.when(c == 0)
    def _():
        signal(barrier, {"tile": sib})
    for k in range(n_half):
        there = lax.rem(x + k, n_half)
        if k == 0:
            pl.when(c != 0)(lambda: signal(barrier, {"tile": 0}))
        else:
            signal(barrier, {"half": there, "tile": 0})

    small = [
        pltpu.make_async_copy(src, dst, small_sem.at[i])
        for i, (src, dst) in enumerate(
            ((left_map, map_l), (right_map, map_r), (branch_bits, branch_v), (cut_side, side_v))
        )
    ]
    top, bottom = left_layer.at[pl.ds(0, sent)], left_layer.at[pl.ds(sent, kept)]
    own_left = pltpu.make_async_copy(left_prefix, left_rows.at[x, z], own_sem.at[0])
    own_layer = [
        pltpu.make_async_copy(top, left_w.at[own_sent(c)], own_sem.at[1]),
        pltpu.make_async_copy(bottom, left_w.at[own_kept(c)], own_sem.at[2]),
    ]
    own_weights = pltpu.make_async_copy(right_layer, right_w, own_sem.at[3])
    own_right = pltpu.make_async_copy(right_prefix, right_rows.at[z, mine], own_sem.at[4])
    own_left.start()
    pl.when(is_hub)(own_right.start)
    for copy in small + own_layer + [own_weights]:
        copy.start()

    def prepare():
        for copy in small:
            copy.wait()
        side = spread_sides(side_v[...].astype(jnp.float32))
        branch = branch_v[...].astype(jnp.float32)
        hot_l[...] = one_hot(hot_l.shape[1], map_l[...])
        write_factor(left_factor, branch, side)
        hot_r[...] = one_hot(hot_r.shape[1], map_r[...])
        write_factor(right_factor, branch, 1.0 - side)

    def gather_out(there):
        return remote(
            right_prefix, right_rows.at[z, mine], rg_send.at[there], rg_recv.at[mine],
            {"half": there, "tile": hub},
        )

    def gather_in(owner):
        held = right_rows.at[z, owner]
        return remote(held, held, rg_send.at[0], rg_recv.at[owner], {"tile": sib})

    def weights_out(k):
        return remote(
            top, left_w.at[other_sent(k, c)], w_send.at[k], w_recv.at[k], {"half": to_x(k)}
        )

    def weights_in(k):
        held = left_w.at[other_sent(k, c)]
        return remote(held, held, w_send.at[k], w_recv.at[k], {"tile": sib})

    def weights_share(k, core):
        held = left_w.at[other_sent(k, core)]
        return remote(held, held, ws_send.at[k], ws_recv.at[k], {"tile": sib})

    def layer_share(core):
        return [
            remote(part, left_w.at[where], o_send.at[i], o_recv.at[i], {"tile": sib})
            for i, (part, where) in enumerate(((top, own_sent(core)), (bottom, own_kept(core))))
        ]

    def left_out(there):
        return remote(
            left_prefix, left_rows.at[x, z], lp_send.at[there], lp_recv.at[z], {"path": there}
        )

    def left_in(block):
        held = left_rows.at[x, block]
        return remote(held, held, lp_send.at[block], lp_recv.at[block], {"path": block})

    def left_on(k):
        return remote(left_rows.at[x], left_rows.at[x], lx_send.at[k], lx_recv.at[k], {"half": to_x(k)})

    def left_over(k):
        held = left_rows.at[to_x(k)]
        back = n_half - 2 - k
        return remote(held, held, lx_send.at[back], lx_recv.at[back], {"half": to_x(k)})

    def blocks_out(there):
        return remote(right_rows.at[z], right_rows.at[z], rz_send.at[there], rz_recv.at[z], {"path": there})

    def blocks_in(block):
        held = right_rows.at[block]
        return remote(held, held, rz_send.at[block], rz_recv.at[block], {"path": block})

    def states_out(block):
        return remote(
            right_stage.at[block // n_tile], right_st.at[at_r(z)], st_send.at[block], st_recv.at[z], {"path": block}
        )

    def states_in(block):
        held = right_st.at[at_r(block)]
        return remote(held, held, st_send.at[block], st_recv.at[block], {"path": block})

    def states_share(block):
        held = right_st.at[at_r(block)]
        return remote(held, held, ss_send.at[block], ss_recv.at[block], {"tile": sib})

    def left_states_out(k):
        return remote(
            left_stage.at[k], left_st.at[other_kept(k)], ls_send.at[k], ls_recv.at[k], {"half": to_x(k)}
        )

    def left_states_in(k):
        held = left_st.at[other_kept(k)]
        return remote(held, held, ls_send.at[k], ls_recv.at[k], {"half": to_x(k)})

    def in_plane():
        @pl.when(c == 0)
        def _():
            pl.semaphore_wait(barrier, n_lr - 1)
            signal(near_sem, {"tile": sib})
        @pl.when(c != 0)
        def _():
            pl.semaphore_wait(near_sem, 1)
        for k in range(n_half):
            if k == 0:
                pl.when(jnp.logical_not(is_hub))(gather_out(x).start)
            else:
                gather_out(lax.rem(x + k, n_half)).start()
        for k in range(n_half - 1):
            weights_out(k).start()
        for copy in layer_share(c):
            copy.start()

    def in_column():
        @pl.when(c != 0)
        def _():
            pl.semaphore_wait(barrier, (n_path - 1) * n_tile + 1)
            signal(far_sem, {"tile": sib})
        @pl.when(c == 0)
        def _():
            pl.semaphore_wait(far_sem, 1)
        others(n_path, z, lambda there: left_out(there).start())

    @pl.when(early)
    def _():
        in_plane()
        prepare()
        in_column()
    @pl.when(late)
    def _():
        in_column()
        in_plane()
        prepare()

    @pl.when(is_hub)
    def _():
        own_right.wait()
        others(n_lr, mine, lambda owner: gather_in(owner).wait_recv())
        others(n_path, z, lambda there: blocks_out(there).start())

    own_left.wait()
    others(n_path, z, lambda block: left_in(block).wait_recv())
    for k in range(n_half - 1):
        left_on(k).start()
    project(own_proj, hot_l, left_rows[x], left_factor)
    for copy in own_layer:
        copy.wait()
    for copy in layer_share(sib):
        copy.wait_recv()
    left_st[0:chip_l, :] = nt(left_w[0:chip_l, :], own_proj[...])

    own_weights.wait()
    first = jnp.where(is_hub, z // n_tile + 1, 0)
    def form_right(j):
        block = lax.rem(first + j, per_core) * n_tile + c
        @pl.when(block != z)
        def _():
            blocks_in(block).wait_recv()
        project(proj, hot_r, right_rows[block], right_factor)
        states = nt(right_w[...], proj[...])
        @pl.when(block != z)
        def _():
            right_stage[block // n_tile] = states
            states_out(block).start()
        @pl.when(block == z)
        def _():
            right_st[at_r(z), :] = states
            states_share(z).start()

    def form_left(k):
        left_over(k).wait_recv()
        project(proj, hot_l, left_rows[to_x(k)], left_factor)
        left_stage[k] = nt(left_w[n_tile * sent:chip_l, :], proj[...])
        left_states_out(k).start()

    pl.when(late)(lambda: loop(per_core, form_right))
    loop(n_half - 1, form_left)
    pl.when(early)(lambda: loop(per_core, form_right))

    def take_weights(k):
        weights_in(k).wait_recv()
        weights_share(k, c).start()
    loop(n_half - 1, take_weights)
    loop(n_half - 1, lambda k: weights_share(k, sib).wait_recv())
    if n_half > 1:
        left_st[chip_l:known, :] = nt(left_w[chip_l:known, :], own_proj[...])

    unit = max(block_r, 128)
    in_unit = unit // block_r
    n_units = n_path // in_unit

    def right_ready(block):
        @pl.when(is_hub)
        def _():
            @pl.when(block != z)
            def _():
                states_in(block).wait_recv()
                states_share(block).start()
        @pl.when(jnp.logical_not(is_hub))
        def _():
            states_share(block).wait_recv()

    def put(cols, owner, start, value):
        out[span(owner * block_l + start, value.shape[0]), cols] = value

    def take_right(u):
        at = lax.rem(z // in_unit + u, n_units)
        for i in range(in_unit):
            right_ready(at * in_unit + i)
        cols = pl.ds(pl.multiple_of(at * unit, 128), unit)
        made = nt(left_st[0:known, :], right_st[span(at * unit, unit), :])
        for core in range(n_tile):
            put(cols, x * n_tile + core, 0, made[core * sent:(core + 1) * sent])
            low = n_tile * sent + core * kept
            put(cols, x * n_tile + core, sent, made[low:low + kept])
            for k in range(n_half - 1):
                low = chip_l + (k * n_tile + core) * sent
                put(cols, from_x(k) * n_tile + core, 0, made[low:low + sent])
    loop(n_units, take_right)

    def take_left(k):
        left_states_in(k).wait_recv()
        made = nt(left_st[other_kept(k), :], right_st[...])
        for core in range(n_tile):
            put(slice(None), from_x(k) * n_tile + core, sent, made[core * kept:(core + 1) * kept])
    loop(n_half - 1, take_left)

    others(n_path, z, lambda there: left_out(there).wait_send())
    def gather_gone(there):
        @pl.when(jnp.logical_or(there != x, jnp.logical_not(is_hub)))
        def _():
            gather_out(there).wait_send()
    loop(n_half, gather_gone)
    for copy in layer_share(c):
        copy.wait_send()
    def x_gone(k):
        weights_out(k).wait_send()
        weights_share(k, c).wait_send()
        left_on(k).wait_send()
        left_states_out(k).wait_send()
    loop(n_half - 1, x_gone)
    def right_gone(j):
        block = j * n_tile + c
        @pl.when(block != z)
        def _():
            states_out(block).wait_send()
    loop(per_core, right_gone)
    @pl.when(is_hub)
    def _():
        loop(n_path, lambda block: states_share(block).wait_send())
        others(n_path, z, lambda there: blocks_out(there).wait_send())


def on_device(
    sizes,
    left_prefix, right_prefix, left_layer, right_layer, left_map, right_map, branch_bits, cut_side,
):
    n_half, n_path, n_tile = sizes
    n_lr = n_half * n_tile
    paths = left_map.shape[0]
    cuts = cut_side.shape[0]
    block_l, gate = left_layer.shape
    block_r = right_layer.shape[0]
    rows_l, rows_r = block_l * n_lr, block_r * n_path
    sent = sent_rows(block_l)
    kept = block_l - sent
    known = n_tile * (block_l + (n_half - 1) * sent)
    many = max(1, n_half - 1)
    dma = pltpu.SemaphoreType.DMA
    bf16, i32 = jnp.bfloat16, jnp.int32
    hbm = pl.BlockSpec(memory_space=pltpu.HBM)
    return pl.pallas_call(
        functools.partial(kernel, sizes),
        out_shape=jax.ShapeDtypeStruct((rows_l, rows_r), bf16),
        in_specs=[hbm] * 8,
        out_specs=pl.BlockSpec(memory_space=pltpu.VMEM),
        scratch_shapes=[
            pltpu.VMEM((1, paths), i32), pltpu.VMEM((1, paths), i32),
            pltpu.VMEM((cuts, paths), i32), pltpu.VMEM((1, cuts), i32),
            pltpu.VMEM((n_half, n_path) + left_prefix.shape, bf16),
            pltpu.VMEM((n_path, n_lr) + right_prefix.shape, bf16),
            pltpu.VMEM((paths, gate), bf16), pltpu.VMEM((paths, gate), bf16),
            pltpu.VMEM((paths, gate), bf16), pltpu.VMEM((paths, gate), bf16),
            pltpu.VMEM((known, gate), bf16), pltpu.VMEM((block_r, gate), bf16),
            pltpu.VMEM((rows_l, paths), bf16), pltpu.VMEM((rows_r, paths), bf16),
            pltpu.VMEM((many, n_tile * kept, paths), bf16),
            pltpu.VMEM((n_path // n_tile, block_r, paths), bf16),
            pltpu.VMEM((paths, left_prefix.shape[0] * n_path), bf16),
            pltpu.VMEM((paths, right_prefix.shape[0] * n_lr), bf16),
            pltpu.SemaphoreType.REGULAR, pltpu.SemaphoreType.REGULAR, dma((4,)), dma((5,)),
            dma((2,)), dma((2,)), dma((n_path,)), dma((n_path,)), dma((many,)), dma((many,)),
            dma((n_half,)), dma((n_lr,)), dma((n_path,)), dma((n_path,)),
            dma((many,)), dma((many,)), dma((many,)), dma((many,)),
            dma((n_path,)), dma((n_path,)), dma((n_path,)), dma((n_path,)),
            dma((many,)), dma((many,)),
        ],
        compiler_params=pltpu.CompilerParams(
            collective_id=0, has_side_effects=True, vmem_limit_bytes=40 * 2**20
        ),
    )(*(
        pltpu.with_memory_space_constraint(array, pltpu.HBM) for array in (
            left_prefix, right_prefix, left_layer, right_layer,
            left_map[None, :], right_map[None, :], branch_bits.T, cut_side[None, :],
        )
    ))


def solution(mesh):
    in_specs = (
        P(("groups", "path"), ("half", "tile")),
        P(("groups", "half", "tile"), "path"),
        P(("groups", "half", "tile"), None),
        P(("groups", "path"), None),
        P("groups"),
        P("groups"),
        P("groups", None),
        P("groups"),
    )
    out_specs = P(("groups", "half", "tile"), "path")
    sizes = tuple(mesh.shape[axis] for axis in ("half", "path", "tile"))
    return jax.shard_map(
        functools.partial(on_device, sizes),
        mesh=mesh, in_specs=in_specs, out_specs=out_specs, check_vma=False,
    )
```

```python
import functools

import jax
import jax.numpy as jnp
from jax import lax
from jax.experimental import pallas as pl
from jax.experimental.pallas import tpu as pltpu
from jax.sharding import PartitionSpec as P

MESH = pl.DeviceIdType.MESH
NT = (((1,), (1,)), ((), ()))
TN = (((0,), (0,)), ((), ()))
FULL_MISS = 64.0
CHUNKS = 4


def chunk_rows(block):
    return max(16, block // CHUNKS // 16 * 16)


def spread_sides(side_row):
    cuts = side_row.shape[1]
    across = lax.broadcasted_iota(jnp.int32, (cuts, cuts), 0)
    down = lax.broadcasted_iota(jnp.int32, (cuts, cuts), 1)
    return jnp.sum(jnp.where(across == down, side_row, 0.0), axis=1, keepdims=True)


def write_factor(dst, branch, projector):
    cuts, gate = branch.shape[0], dst.shape[1]
    chosen = branch * projector
    table = jnp.concatenate(
        [FULL_MISS * chosen, FULL_MISS * (projector - chosen) + (branch - chosen)], axis=0
    ).astype(jnp.bfloat16)
    width = min(256, gate)
    for at in range(0, gate, width):
        place = lax.broadcasted_iota(jnp.int32, (cuts, width), 0)
        code = lax.broadcasted_iota(jnp.int32, (cuts, width), 1) + at
        bits = (jnp.right_shift(code, place) & 1).astype(jnp.float32)
        both = jnp.concatenate([1.0 - bits, bits], axis=0).astype(jnp.bfloat16)
        count = lax.dot_general(
            table, both, TN, preferred_element_type=jnp.float32
        ).astype(jnp.int32)
        sign = (1 - 2 * (count & 1)).astype(jnp.float32)
        dst[:, at:at + width] = jnp.where(count < int(FULL_MISS), sign, 0.0).astype(jnp.bfloat16)


def one_hot(rows, path_map):
    which = lax.broadcasted_iota(jnp.int32, (rows, path_map.shape[1]), 0)
    return jnp.where(which == path_map, 1.0, 0.0).T.astype(jnp.bfloat16)


def project(dst, hot, prefix, factor):
    gate = prefix.shape[-1]
    rows = prefix.astype(jnp.float32).reshape(-1, gate).astype(jnp.bfloat16)
    picks = hot[...]
    width = min(256, gate)
    for at in range(0, gate, width):
        chosen = jnp.dot(picks, rows[:, at:at + width], preferred_element_type=jnp.float32)
        dst[:, at:at + width] = chosen.astype(jnp.bfloat16) * factor[:, at:at + width]


def nt(a, b):
    return lax.dot_general(a, b, NT, preferred_element_type=jnp.float32).astype(jnp.bfloat16)


def kernel(
    sizes,
    left_prefix, right_prefix, left_layer, right_layer, left_map, right_map, branch_bits, cut_side,
    out,
    map_l, map_r, branch_v, side_v,
    left_rows, right_rows, left_factor, right_factor, own_proj, proj, left_w, right_w,
    left_st, right_st, right_stage, hot_l, hot_r,
    near_sem, far_sem, small_sem, own_sem,
    o_send, o_recv, lp_send, lp_recv, rg_send, rg_recv, rz_send, rz_recv,
    w_send, w_recv, ws_send, ws_recv, st_send, st_recv, ss_send, ss_recv,
):
    n_half, n_path, n_tile = sizes
    x, z, c = lax.axis_index("half"), lax.axis_index("path"), lax.axis_index("tile")
    sib = 1 - c
    n_lr = n_half * n_tile
    mine = x * n_tile + c
    block_l, gate = left_layer.shape
    block_r = right_layer.shape[0]
    chunk = chunk_rows(block_l)
    count = block_l // chunk
    chip_l = n_tile * block_l
    hub = lax.rem(z, n_tile)
    is_hub = c == hub
    per_core = n_path // n_tile
    early = z * 2 < n_path
    late = jnp.logical_not(early)

    barrier = pltpu.get_barrier_semaphore()

    def loop(n, do):
        if n == 1:
            do(0)
        elif n > 1:
            lax.fori_loop(0, n, lambda t, _: (do(t), 0)[1], 0)

    def others(n, me, do):
        def step(t):
            pl.when(t != me)(lambda: do(t))
        loop(n, step)

    def remote(src, dst, send, recv, device):
        return pltpu.make_async_remote_copy(
            src_ref=src, dst_ref=dst, send_sem=send, recv_sem=recv, device_id=device, device_id_type=MESH
        )

    def signal(sem, device):
        pl.semaphore_signal(sem, inc=1, device_id=device, device_id_type=MESH)

    def span(start, rows):
        return pl.ds(start if isinstance(start, int) else pl.multiple_of(start, 16), rows)

    def own_rows(core):
        return span(core * block_l, block_l)

    def other_rows(k, i, core):
        return span(chip_l + ((i * (n_half - 1) + k) * n_tile + core) * chunk, chunk)

    def at_r(block):
        return span(block * block_r, block_r)

    def to_x(k):
        return lax.rem(x + k + 1, n_half)

    def from_x(k):
        return lax.rem(x + n_half - k - 1, n_half)

    def greet_column(t):
        there = lax.rem(z + 1 + t, n_path)
        signal(barrier, {"path": there, "tile": lax.rem(there, n_tile)})

    loop(n_path - 1, greet_column)
    signal(barrier, {"tile": sib})
    for k in range(n_half - 1):
        signal(barrier, {"half": to_x(k), "tile": 1 - hub})

    small = [
        pltpu.make_async_copy(src, dst, small_sem.at[i])
        for i, (src, dst) in enumerate(
            ((left_map, map_l), (right_map, map_r), (branch_bits, branch_v), (cut_side, side_v))
        )
    ]
    own_left = pltpu.make_async_copy(left_prefix, left_rows.at[z], own_sem.at[0])
    own_layer = pltpu.make_async_copy(left_layer, left_w.at[own_rows(c)], own_sem.at[1])
    own_weights = pltpu.make_async_copy(right_layer, right_w, own_sem.at[2])
    own_right = pltpu.make_async_copy(right_prefix, right_rows.at[z, mine], own_sem.at[3])
    own_left.start()
    pl.when(is_hub)(own_right.start)
    for copy in small + [own_layer, own_weights]:
        copy.start()

    def prepare():
        for copy in small:
            copy.wait()
        side = spread_sides(side_v[...].astype(jnp.float32))
        branch = branch_v[...].astype(jnp.float32)
        hot_l[...] = one_hot(hot_l.shape[1], map_l[...])
        write_factor(left_factor, branch, side)
        hot_r[...] = one_hot(hot_r.shape[1], map_r[...])
        write_factor(right_factor, branch, 1.0 - side)

    def gather_out(there):
        return remote(
            right_prefix, right_rows.at[z, mine], rg_send.at[there], rg_recv.at[mine],
            {"half": there, "tile": hub},
        )

    def gather_in(owner):
        held = right_rows.at[z, owner]
        return remote(held, held, rg_send.at[0], rg_recv.at[owner], {"tile": sib})

    def weights_out(k, i):
        return remote(
            left_layer.at[pl.ds(i * chunk, chunk)], left_w.at[other_rows(k, i, c)],
            w_send.at[k, i], w_recv.at[k, i], {"half": to_x(k)},
        )

    def weights_in(k, i):
        held = left_w.at[other_rows(k, i, c)]
        return remote(held, held, w_send.at[k, i], w_recv.at[k, i], {"tile": sib})

    def weights_share(k, i, core):
        held = left_w.at[other_rows(k, i, core)]
        return remote(held, held, ws_send.at[k, i], ws_recv.at[k, i], {"tile": sib})

    def layer_share(core):
        return remote(left_layer, left_w.at[own_rows(core)], o_send.at[0], o_recv.at[0], {"tile": sib})

    def left_out(there):
        return remote(
            left_prefix, left_rows.at[z], lp_send.at[there], lp_recv.at[z], {"path": there}
        )

    def left_in(block):
        held = left_rows.at[block]
        return remote(held, held, lp_send.at[block], lp_recv.at[block], {"path": block})

    def blocks_out(there):
        return remote(right_rows.at[z], right_rows.at[z], rz_send.at[there], rz_recv.at[z], {"path": there})

    def blocks_in(block):
        held = right_rows.at[block]
        return remote(held, held, rz_send.at[block], rz_recv.at[block], {"path": block})

    def states_out(block):
        return remote(
            right_stage.at[block // n_tile], right_st.at[at_r(z)], st_send.at[block], st_recv.at[z], {"path": block}
        )

    def states_in(block):
        held = right_st.at[at_r(block)]
        return remote(held, held, st_send.at[block], st_recv.at[block], {"path": block})

    def states_share(block):
        held = right_st.at[at_r(block)]
        return remote(held, held, ss_send.at[block], ss_recv.at[block], {"tile": sib})

    def in_plane():
        @pl.when(jnp.logical_not(is_hub))
        def _():
            pl.semaphore_wait(barrier, n_lr - 1)
            signal(near_sem, {"tile": sib})
        @pl.when(is_hub)
        def _():
            pl.semaphore_wait(near_sem, 1)
        for k in range(n_half):
            if k == 0:
                pl.when(jnp.logical_not(is_hub))(gather_out(x).start)
            else:
                gather_out(lax.rem(x + k, n_half)).start()
        for i in range(count):
            for k in range(n_half - 1):
                weights_out(k, i).start()
        layer_share(c).start()

    def in_column():
        @pl.when(is_hub)
        def _():
            pl.semaphore_wait(barrier, (n_path - 1) * n_tile + 1)
            signal(far_sem, {"tile": sib})
        @pl.when(jnp.logical_not(is_hub))
        def _():
            pl.semaphore_wait(far_sem, 1)

    def spread(do):
        def step(t):
            d = n_path - 1 - t
            pl.when(z >= d)(lambda: do(z - d))
            pl.when(z + d < n_path)(lambda: do(z + d))
        loop(n_path - 1, step)

    def send_blocks():
        @pl.when(is_hub)
        def _():
            own_right.wait()
            others(n_lr, mine, lambda owner: gather_in(owner).wait_recv())
            spread(lambda there: blocks_out(there).start())

    def send_left():
        spread(lambda there: left_out(there).start())

    @pl.when(early)
    def _():
        in_plane()
        prepare()
        in_column()
        send_blocks()
        send_left()
    @pl.when(late)
    def _():
        in_column()
        in_plane()
        prepare()
        send_blocks()
        send_left()

    own_weights.wait()
    first = jnp.where(is_hub, z // n_tile + 1, 0)
    def form_right(j):
        block = lax.rem(first + j, per_core) * n_tile + c
        @pl.when(block != z)
        def _():
            blocks_in(block).wait_recv()
        project(proj, hot_r, right_rows[block], right_factor)
        states = nt(right_w[...], proj[...])
        @pl.when(block != z)
        def _():
            right_stage[block // n_tile] = states
            states_out(block).start()
        @pl.when(block == z)
        def _():
            right_st[at_r(z), :] = states
            states_share(z).start()

    loop(per_core, form_right)

    own_left.wait()
    others(n_path, z, lambda block: left_in(block).wait_recv())
    project(own_proj, hot_l, left_rows[...], left_factor)
    own_layer.wait()
    layer_share(sib).wait_recv()
    left_st[0:chip_l, :] = nt(left_w[0:chip_l, :], own_proj[...])

    def pass_weights(i):
        for k in range(n_half - 1):
            weights_in(k, i).wait_recv()
            weights_share(k, i, c).start()

    if n_half > 1:
        loop(count, pass_weights)
        def shared(i):
            for k in range(n_half - 1):
                weights_share(k, i, sib).wait_recv()
        loop(count, shared)
        left_st[chip_l:, :] = nt(left_w[chip_l:, :], own_proj[...])

    unit = max(block_r, 128)
    in_unit = unit // block_r
    n_units = n_path // in_unit

    def right_ready(block):
        @pl.when(is_hub)
        def _():
            @pl.when(block != z)
            def _():
                states_in(block).wait_recv()
                states_share(block).start()
        @pl.when(jnp.logical_not(is_hub))
        def _():
            states_share(block).wait_recv()

    def put(cols, owner, start, value):
        out[span(owner * block_l + start, value.shape[0]), cols] = value

    def take_right(u):
        at = lax.rem(z // in_unit + u, n_units)
        for i in range(in_unit):
            right_ready(at * in_unit + i)
        cols = pl.ds(pl.multiple_of(at * unit, 128), unit)
        made = nt(left_st[...], right_st[span(at * unit, unit), :])
        out[span(x * chip_l, chip_l), cols] = made[:chip_l]
        for k in range(n_half - 1):
            for core in range(n_tile):
                for i in range(count):
                    low = chip_l + ((i * (n_half - 1) + k) * n_tile + core) * chunk
                    put(cols, from_x(k) * n_tile + core, i * chunk, made[low:low + chunk])
    loop(n_units, take_right)

    others(n_path, z, lambda there: left_out(there).wait_send())
    def gather_gone(there):
        @pl.when(jnp.logical_or(there != x, jnp.logical_not(is_hub)))
        def _():
            gather_out(there).wait_send()
    loop(n_half, gather_gone)
    layer_share(c).wait_send()
    for k in range(n_half - 1):
        for i in range(count):
            weights_out(k, i).wait_send()
            weights_share(k, i, c).wait_send()
    def right_gone(j):
        block = j * n_tile + c
        @pl.when(block != z)
        def _():
            states_out(block).wait_send()
    loop(per_core, right_gone)
    @pl.when(is_hub)
    def _():
        loop(n_path, lambda block: states_share(block).wait_send())
        others(n_path, z, lambda there: blocks_out(there).wait_send())


def on_device(
    sizes,
    left_prefix, right_prefix, left_layer, right_layer, left_map, right_map, branch_bits, cut_side,
):
    n_half, n_path, n_tile = sizes
    n_lr = n_half * n_tile
    paths = left_map.shape[0]
    cuts = cut_side.shape[0]
    block_l, gate = left_layer.shape
    block_r = right_layer.shape[0]
    rows_l, rows_r = block_l * n_lr, block_r * n_path
    count = block_l // chunk_rows(block_l)
    many = max(1, n_half - 1)
    dma = pltpu.SemaphoreType.DMA
    bf16, i32 = jnp.bfloat16, jnp.int32
    hbm = pl.BlockSpec(memory_space=pltpu.HBM)
    return pl.pallas_call(
        functools.partial(kernel, sizes),
        out_shape=jax.ShapeDtypeStruct((rows_l, rows_r), bf16),
        in_specs=[hbm] * 8,
        out_specs=pl.BlockSpec(memory_space=pltpu.VMEM),
        scratch_shapes=[
            pltpu.VMEM((1, paths), i32), pltpu.VMEM((1, paths), i32),
            pltpu.VMEM((cuts, paths), i32), pltpu.VMEM((1, cuts), i32),
            pltpu.VMEM((n_path,) + left_prefix.shape, bf16),
            pltpu.VMEM((n_path, n_lr) + right_prefix.shape, bf16),
            pltpu.VMEM((paths, gate), bf16), pltpu.VMEM((paths, gate), bf16),
            pltpu.VMEM((paths, gate), bf16), pltpu.VMEM((paths, gate), bf16),
            pltpu.VMEM((rows_l, gate), bf16), pltpu.VMEM((block_r, gate), bf16),
            pltpu.VMEM((rows_l, paths), bf16), pltpu.VMEM((rows_r, paths), bf16),
            pltpu.VMEM((n_path // n_tile, block_r, paths), bf16),
            pltpu.VMEM((paths, left_prefix.shape[0] * n_path), bf16),
            pltpu.VMEM((paths, right_prefix.shape[0] * n_lr), bf16),
            pltpu.SemaphoreType.REGULAR, pltpu.SemaphoreType.REGULAR, dma((4,)), dma((4,)),
            dma((1,)), dma((1,)), dma((n_path,)), dma((n_path,)),
            dma((n_half,)), dma((n_lr,)), dma((n_path,)), dma((n_path,)),
            dma((many, count)), dma((many, count)), dma((many, count)), dma((many, count)),
            dma((n_path,)), dma((n_path,)), dma((n_path,)), dma((n_path,)),
        ],
        compiler_params=pltpu.CompilerParams(
            collective_id=0, has_side_effects=True, vmem_limit_bytes=40 * 2**20
        ),
    )(*(
        pltpu.with_memory_space_constraint(array, pltpu.HBM) for array in (
            left_prefix, right_prefix, left_layer, right_layer,
            left_map[None, :], right_map[None, :], branch_bits.T, cut_side[None, :],
        )
    ))


def solution(mesh):
    in_specs = (
        P(("groups", "path"), ("half", "tile")),
        P(("groups", "half", "tile"), "path"),
        P(("groups", "half", "tile"), None),
        P(("groups", "path"), None),
        P("groups"),
        P("groups"),
        P("groups", None),
        P("groups"),
    )
    out_specs = P(("groups", "half", "tile"), "path")
    sizes = tuple(mesh.shape[axis] for axis in ("half", "path", "tile"))
    return jax.shard_map(
        functools.partial(on_device, sizes),
        mesh=mesh, in_specs=in_specs, out_specs=out_specs, check_vma=False,
    )
```

```python
import functools

import jax
import jax.numpy as jnp
from jax import lax
from jax.experimental import pallas as pl
from jax.experimental.pallas import tpu as pltpu
from jax.sharding import PartitionSpec as P

MESH = pl.DeviceIdType.MESH
NT = (((1,), (1,)), ((), ()))
TN = (((0,), (0,)), ((), ()))
FULL_MISS = 64.0
CHUNKS = 4


def chunk_rows(block):
    return max(16, block // CHUNKS // 16 * 16)


def spread_sides(side_row):
    cuts = side_row.shape[1]
    across = lax.broadcasted_iota(jnp.int32, (cuts, cuts), 0)
    down = lax.broadcasted_iota(jnp.int32, (cuts, cuts), 1)
    return jnp.sum(jnp.where(across == down, side_row, 0.0), axis=1, keepdims=True)


def write_factor(dst, branch, projector):
    cuts, gate = branch.shape[0], dst.shape[1]
    chosen = branch * projector
    table = jnp.concatenate(
        [FULL_MISS * chosen, FULL_MISS * (projector - chosen) + (branch - chosen)], axis=0
    ).astype(jnp.bfloat16)
    width = min(256, gate)
    for at in range(0, gate, width):
        place = lax.broadcasted_iota(jnp.int32, (cuts, width), 0)
        code = lax.broadcasted_iota(jnp.int32, (cuts, width), 1) + at
        bits = (jnp.right_shift(code, place) & 1).astype(jnp.float32)
        both = jnp.concatenate([1.0 - bits, bits], axis=0).astype(jnp.bfloat16)
        count = lax.dot_general(
            table, both, TN, preferred_element_type=jnp.float32
        ).astype(jnp.int32)
        sign = (1 - 2 * (count & 1)).astype(jnp.float32)
        dst[:, at:at + width] = jnp.where(count < int(FULL_MISS), sign, 0.0).astype(jnp.bfloat16)


def one_hot(rows, path_map):
    which = lax.broadcasted_iota(jnp.int32, (rows, path_map.shape[1]), 0)
    return jnp.where(which == path_map, 1.0, 0.0).T.astype(jnp.bfloat16)


def project(dst, hot, prefix, factor):
    gate = prefix.shape[-1]
    rows = prefix.astype(jnp.float32).reshape(-1, gate).astype(jnp.bfloat16)
    picks = hot[...]
    width = min(256, gate)
    for at in range(0, gate, width):
        chosen = jnp.dot(picks, rows[:, at:at + width], preferred_element_type=jnp.float32)
        dst[:, at:at + width] = chosen.astype(jnp.bfloat16) * factor[:, at:at + width]


def nt(a, b):
    return lax.dot_general(a, b, NT, preferred_element_type=jnp.float32).astype(jnp.bfloat16)


def kernel(
    sizes,
    left_prefix, right_prefix, left_layer, right_layer, left_map, right_map, branch_bits, cut_side,
    out,
    map_l, map_r, branch_v, side_v,
    left_rows, right_rows, left_factor, right_factor, own_proj, proj, left_w, right_w,
    left_st, right_st, right_stage, hot_l, hot_r,
    near_sem, far_sem, small_sem, own_sem,
    o_send, o_recv, lp_send, lp_recv, rg_send, rg_recv, rz_send, rz_recv,
    w_send, w_recv, ws_send, ws_recv, st_send, st_recv, ss_send, ss_recv,
):
    n_half, n_path, n_tile = sizes
    x, z, c = lax.axis_index("half"), lax.axis_index("path"), lax.axis_index("tile")
    sib = 1 - c
    n_lr = n_half * n_tile
    mine = x * n_tile + c
    block_l, gate = left_layer.shape
    block_r = right_layer.shape[0]
    chunk = chunk_rows(block_l)
    count = block_l // chunk
    chip_l = n_tile * block_l
    hub = lax.rem(z, n_tile)
    is_hub = c == hub
    per_core = n_path // n_tile
    early = z * 2 < n_path
    late = jnp.logical_not(early)

    barrier = pltpu.get_barrier_semaphore()

    def loop(n, do):
        if n == 1:
            do(0)
        elif n > 1:
            lax.fori_loop(0, n, lambda t, _: (do(t), 0)[1], 0)

    def others(n, me, do):
        def step(t):
            pl.when(t != me)(lambda: do(t))
        loop(n, step)

    def remote(src, dst, send, recv, device):
        return pltpu.make_async_remote_copy(
            src_ref=src, dst_ref=dst, send_sem=send, recv_sem=recv, device_id=device, device_id_type=MESH
        )

    def signal(sem, device):
        pl.semaphore_signal(sem, inc=1, device_id=device, device_id_type=MESH)

    def span(start, rows):
        return pl.ds(start if isinstance(start, int) else pl.multiple_of(start, 16), rows)

    def own_rows(core):
        return span((x * n_tile + core) * block_l, block_l)

    def chunk_of(owner, i):
        return span(owner * block_l + i * chunk, chunk)

    def at_r(block):
        return span(block * block_r, block_r)

    def to_x(k):
        return lax.rem(x + k + 1, n_half)

    def from_x(k):
        return lax.rem(x + n_half - k - 1, n_half)

    def greet_column(t):
        there = lax.rem(z + 1 + t, n_path)
        signal(barrier, {"path": there, "tile": lax.rem(there, n_tile)})

    loop(n_path - 1, greet_column)
    signal(barrier, {"tile": sib})
    for k in range(n_half - 1):
        signal(barrier, {"half": to_x(k), "tile": 1 - hub})

    small = [
        pltpu.make_async_copy(src, dst, small_sem.at[i])
        for i, (src, dst) in enumerate(
            ((left_map, map_l), (right_map, map_r), (branch_bits, branch_v), (cut_side, side_v))
        )
    ]
    own_left = pltpu.make_async_copy(left_prefix, left_rows.at[z], own_sem.at[0])
    own_layer = pltpu.make_async_copy(left_layer, left_w.at[own_rows(c)], own_sem.at[1])
    own_weights = pltpu.make_async_copy(right_layer, right_w, own_sem.at[2])
    own_right = pltpu.make_async_copy(right_prefix, right_rows.at[z, mine], own_sem.at[3])
    own_left.start()
    pl.when(is_hub)(own_right.start)
    for copy in small + [own_layer, own_weights]:
        copy.start()

    def prepare():
        for copy in small:
            copy.wait()
        side = spread_sides(side_v[...].astype(jnp.float32))
        branch = branch_v[...].astype(jnp.float32)
        hot_l[...] = one_hot(hot_l.shape[1], map_l[...])
        write_factor(left_factor, branch, side)
        hot_r[...] = one_hot(hot_r.shape[1], map_r[...])
        write_factor(right_factor, branch, 1.0 - side)

    def gather_out(there):
        return remote(
            right_prefix, right_rows.at[z, mine], rg_send.at[there], rg_recv.at[mine],
            {"half": there, "tile": hub},
        )

    def gather_in(owner):
        held = right_rows.at[z, owner]
        return remote(held, held, rg_send.at[0], rg_recv.at[owner], {"tile": sib})

    def weights_out(k, i):
        return remote(
            left_layer.at[pl.ds(i * chunk, chunk)], left_w.at[chunk_of(mine, i)],
            w_send.at[k, i], w_recv.at[k, i], {"half": to_x(k)},
        )

    def weights_in(k, i):
        held = left_w.at[chunk_of(from_x(k) * n_tile + c, i)]
        return remote(held, held, w_send.at[k, i], w_recv.at[k, i], {"tile": sib})

    def weights_share(k, i, core):
        held = left_w.at[chunk_of(from_x(k) * n_tile + core, i)]
        return remote(held, held, ws_send.at[k, i], ws_recv.at[k, i], {"tile": sib})

    def layer_share(core):
        return remote(left_layer, left_w.at[own_rows(core)], o_send.at[0], o_recv.at[0], {"tile": sib})

    def left_out(there):
        return remote(
            left_prefix, left_rows.at[z], lp_send.at[there], lp_recv.at[z], {"path": there}
        )

    def left_in(block):
        held = left_rows.at[block]
        return remote(held, held, lp_send.at[block], lp_recv.at[block], {"path": block})

    def blocks_out(there):
        return remote(right_rows.at[z], right_rows.at[z], rz_send.at[there], rz_recv.at[z], {"path": there})

    def blocks_in(block):
        held = right_rows.at[block]
        return remote(held, held, rz_send.at[block], rz_recv.at[block], {"path": block})

    def states_out(block):
        return remote(
            right_stage.at[block // n_tile], right_st.at[at_r(z)], st_send.at[block], st_recv.at[z], {"path": block}
        )

    def states_in(block):
        held = right_st.at[at_r(block)]
        return remote(held, held, st_send.at[block], st_recv.at[block], {"path": block})

    def states_share(block):
        held = right_st.at[at_r(block)]
        return remote(held, held, ss_send.at[block], ss_recv.at[block], {"tile": sib})

    def in_plane():
        @pl.when(jnp.logical_not(is_hub))
        def _():
            pl.semaphore_wait(barrier, n_lr - 1)
            signal(near_sem, {"tile": sib})
        @pl.when(is_hub)
        def _():
            pl.semaphore_wait(near_sem, 1)
        for k in range(n_half):
            if k == 0:
                pl.when(jnp.logical_not(is_hub))(gather_out(x).start)
            else:
                gather_out(lax.rem(x + k, n_half)).start()
        for i in range(count):
            for k in range(n_half - 1):
                weights_out(k, i).start()
        layer_share(c).start()

    def in_column():
        @pl.when(is_hub)
        def _():
            pl.semaphore_wait(barrier, (n_path - 1) * n_tile + 1)
            signal(far_sem, {"tile": sib})
        @pl.when(jnp.logical_not(is_hub))
        def _():
            pl.semaphore_wait(far_sem, 1)

    def spread(do):
        def step(t):
            d = n_path - 1 - t
            pl.when(z >= d)(lambda: do(z - d))
            pl.when(z + d < n_path)(lambda: do(z + d))
        loop(n_path - 1, step)

    def send_blocks():
        @pl.when(is_hub)
        def _():
            own_right.wait()
            others(n_lr, mine, lambda owner: gather_in(owner).wait_recv())
            spread(lambda there: blocks_out(there).start())

    def send_left():
        spread(lambda there: left_out(there).start())

    @pl.when(early)
    def _():
        in_plane()
        prepare()
        in_column()
        send_blocks()
        send_left()
    @pl.when(late)
    def _():
        in_column()
        send_left()
        in_plane()
        prepare()
        send_blocks()

    own_weights.wait()
    first = jnp.where(is_hub, z // n_tile + 1, 0)
    def form_right(j):
        block = lax.rem(first + j, per_core) * n_tile + c
        @pl.when(block != z)
        def _():
            blocks_in(block).wait_recv()
        project(proj, hot_r, right_rows[block], right_factor)
        states = nt(right_w[...], proj[...])
        @pl.when(block != z)
        def _():
            right_stage[block // n_tile] = states
            states_out(block).start()
        @pl.when(block == z)
        def _():
            right_st[at_r(z), :] = states
            states_share(z).start()

    loop(per_core, form_right)

    own_left.wait()
    others(n_path, z, lambda block: left_in(block).wait_recv())
    project(own_proj, hot_l, left_rows[...], left_factor)
    own_layer.wait()
    layer_share(sib).wait_recv()

    def pass_weights(i):
        for k in range(n_half - 1):
            weights_in(k, i).wait_recv()
            weights_share(k, i, c).start()

    def shared(i):
        for k in range(n_half - 1):
            weights_share(k, i, sib).wait_recv()

    def form_rows(t):
        @pl.when(t == 1)
        def _():
            loop(count, pass_weights)
            loop(count, shared)
        rows = span(lax.rem(x + t, n_half) * chip_l, chip_l)
        left_st[rows, :] = nt(left_w[rows, :], own_proj[...])
    loop(n_half, form_rows)

    unit = max(min(2, n_path) * block_r, 128)
    in_unit = unit // block_r
    n_units = n_path // in_unit

    def right_ready(block):
        @pl.when(is_hub)
        def _():
            @pl.when(block != z)
            def _():
                states_in(block).wait_recv()
                states_share(block).start()
        @pl.when(jnp.logical_not(is_hub))
        def _():
            states_share(block).wait_recv()

    def take_right(u):
        at = lax.rem(z // in_unit + u, n_units)
        for i in range(in_unit):
            right_ready(at * in_unit + i)
        cols = pl.ds(pl.multiple_of(at * unit, 128), unit)
        out[:, cols] = nt(left_st[...], right_st[span(at * unit, unit), :])
    loop(n_units, take_right)

    others(n_path, z, lambda there: left_out(there).wait_send())
    def gather_gone(there):
        @pl.when(jnp.logical_or(there != x, jnp.logical_not(is_hub)))
        def _():
            gather_out(there).wait_send()
    loop(n_half, gather_gone)
    layer_share(c).wait_send()
    for k in range(n_half - 1):
        for i in range(count):
            weights_out(k, i).wait_send()
            weights_share(k, i, c).wait_send()
    def right_gone(j):
        block = j * n_tile + c
        @pl.when(block != z)
        def _():
            states_out(block).wait_send()
    loop(per_core, right_gone)
    @pl.when(is_hub)
    def _():
        loop(n_path, lambda block: states_share(block).wait_send())
        others(n_path, z, lambda there: blocks_out(there).wait_send())


def on_device(
    sizes,
    left_prefix, right_prefix, left_layer, right_layer, left_map, right_map, branch_bits, cut_side,
):
    n_half, n_path, n_tile = sizes
    n_lr = n_half * n_tile
    paths = left_map.shape[0]
    cuts = cut_side.shape[0]
    block_l, gate = left_layer.shape
    block_r = right_layer.shape[0]
    rows_l, rows_r = block_l * n_lr, block_r * n_path
    count = block_l // chunk_rows(block_l)
    many = max(1, n_half - 1)
    dma = pltpu.SemaphoreType.DMA
    bf16, i32 = jnp.bfloat16, jnp.int32
    hbm = pl.BlockSpec(memory_space=pltpu.HBM)
    return pl.pallas_call(
        functools.partial(kernel, sizes),
        out_shape=jax.ShapeDtypeStruct((rows_l, rows_r), bf16),
        in_specs=[hbm] * 8,
        out_specs=pl.BlockSpec(memory_space=pltpu.VMEM),
        scratch_shapes=[
            pltpu.VMEM((1, paths), i32), pltpu.VMEM((1, paths), i32),
            pltpu.VMEM((cuts, paths), i32), pltpu.VMEM((1, cuts), i32),
            pltpu.VMEM((n_path,) + left_prefix.shape, bf16),
            pltpu.VMEM((n_path, n_lr) + right_prefix.shape, bf16),
            pltpu.VMEM((paths, gate), bf16), pltpu.VMEM((paths, gate), bf16),
            pltpu.VMEM((paths, gate), bf16), pltpu.VMEM((paths, gate), bf16),
            pltpu.VMEM((rows_l, gate), bf16), pltpu.VMEM((block_r, gate), bf16),
            pltpu.VMEM((rows_l, paths), bf16), pltpu.VMEM((rows_r, paths), bf16),
            pltpu.VMEM((n_path // n_tile, block_r, paths), bf16),
            pltpu.VMEM((paths, left_prefix.shape[0] * n_path), bf16),
            pltpu.VMEM((paths, right_prefix.shape[0] * n_lr), bf16),
            pltpu.SemaphoreType.REGULAR, pltpu.SemaphoreType.REGULAR, dma((4,)), dma((4,)),
            dma((1,)), dma((1,)), dma((n_path,)), dma((n_path,)),
            dma((n_half,)), dma((n_lr,)), dma((n_path,)), dma((n_path,)),
            dma((many, count)), dma((many, count)), dma((many, count)), dma((many, count)),
            dma((n_path,)), dma((n_path,)), dma((n_path,)), dma((n_path,)),
        ],
        compiler_params=pltpu.CompilerParams(
            collective_id=0, has_side_effects=True, vmem_limit_bytes=40 * 2**20
        ),
    )(*(
        pltpu.with_memory_space_constraint(array, pltpu.HBM) for array in (
            left_prefix, right_prefix, left_layer, right_layer,
            left_map[None, :], right_map[None, :], branch_bits.T, cut_side[None, :],
        )
    ))


def solution(mesh):
    in_specs = (
        P(("groups", "path"), ("half", "tile")),
        P(("groups", "half", "tile"), "path"),
        P(("groups", "half", "tile"), None),
        P(("groups", "path"), None),
        P("groups"),
        P("groups"),
        P("groups", None),
        P("groups"),
    )
    out_specs = P(("groups", "half", "tile"), "path")
    sizes = tuple(mesh.shape[axis] for axis in ("half", "path", "tile"))
    return jax.shard_map(
        functools.partial(on_device, sizes),
        mesh=mesh, in_specs=in_specs, out_specs=out_specs, check_vma=False,
    )
```

```python
import functools

import jax
import jax.numpy as jnp
from jax import lax
from jax.experimental import pallas as pl
from jax.experimental.pallas import tpu as pltpu
from jax.sharding import PartitionSpec as P

MESH = pl.DeviceIdType.MESH
NT = (((1,), (1,)), ((), ()))
TN = (((0,), (0,)), ((), ()))
FULL_MISS = 64.0
CHUNKS = 4


def chunk_rows(block):
    return max(16, block // CHUNKS // 16 * 16)


def spread_sides(side_row):
    cuts = side_row.shape[1]
    across = lax.broadcasted_iota(jnp.int32, (cuts, cuts), 0)
    down = lax.broadcasted_iota(jnp.int32, (cuts, cuts), 1)
    return jnp.sum(jnp.where(across == down, side_row, 0.0), axis=1, keepdims=True)


def write_factor(dst, branch, projector):
    cuts, gate = branch.shape[0], dst.shape[1]
    chosen = branch * projector
    table = jnp.concatenate(
        [FULL_MISS * chosen, FULL_MISS * (projector - chosen) + (branch - chosen)], axis=0
    ).astype(jnp.bfloat16)
    width = min(256, gate)
    for at in range(0, gate, width):
        place = lax.broadcasted_iota(jnp.int32, (cuts, width), 0)
        code = lax.broadcasted_iota(jnp.int32, (cuts, width), 1) + at
        bits = (jnp.right_shift(code, place) & 1).astype(jnp.float32)
        both = jnp.concatenate([1.0 - bits, bits], axis=0).astype(jnp.bfloat16)
        count = lax.dot_general(
            table, both, TN, preferred_element_type=jnp.float32
        ).astype(jnp.int32)
        sign = (1 - 2 * (count & 1)).astype(jnp.float32)
        dst[:, at:at + width] = jnp.where(count < int(FULL_MISS), sign, 0.0).astype(jnp.bfloat16)


def one_hot(rows, path_map):
    which = lax.broadcasted_iota(jnp.int32, (rows, path_map.shape[1]), 0)
    return jnp.where(which == path_map, 1.0, 0.0).T.astype(jnp.bfloat16)


def project(dst, hot, prefix, factor):
    gate = prefix.shape[-1]
    rows = prefix.astype(jnp.float32).reshape(-1, gate).astype(jnp.bfloat16)
    picks = hot[...]
    width = min(256, gate)
    for at in range(0, gate, width):
        chosen = jnp.dot(picks, rows[:, at:at + width], preferred_element_type=jnp.float32)
        dst[:, at:at + width] = chosen.astype(jnp.bfloat16) * factor[:, at:at + width]


def nt(a, b):
    return lax.dot_general(a, b, NT, preferred_element_type=jnp.float32).astype(jnp.bfloat16)


def kernel(
    sizes,
    left_prefix, right_prefix, left_layer, right_layer, left_map, right_map, branch_bits, cut_side,
    out,
    map_l, map_r, branch_v, side_v,
    left_rows, right_rows, left_factor, right_factor, own_proj, proj, left_w, right_w,
    left_st, right_st, right_stage, hot_l, hot_r,
    near_sem, far_sem, small_sem, own_sem,
    o_send, o_recv, lp_send, lp_recv, rg_send, rg_recv, rz_send, rz_recv,
    w_send, w_recv, ws_send, ws_recv, st_send, st_recv, ss_send, ss_recv,
):
    n_half, n_path, n_tile = sizes
    x, z, c = lax.axis_index("half"), lax.axis_index("path"), lax.axis_index("tile")
    sib = 1 - c
    n_lr = n_half * n_tile
    mine = x * n_tile + c
    block_l, gate = left_layer.shape
    block_r = right_layer.shape[0]
    chunk = chunk_rows(block_l)
    count = block_l // chunk
    chip_l = n_tile * block_l
    hub = lax.rem(z, n_tile)
    is_hub = c == hub
    per_core = n_path // n_tile
    early = z * 2 < n_path
    late = jnp.logical_not(early)

    barrier = pltpu.get_barrier_semaphore()

    def loop(n, do):
        if n == 1:
            do(0)
        elif n > 1:
            lax.fori_loop(0, n, lambda t, _: (do(t), 0)[1], 0)

    def others(n, me, do):
        def step(t):
            pl.when(t != me)(lambda: do(t))
        loop(n, step)

    def remote(src, dst, send, recv, device):
        return pltpu.make_async_remote_copy(
            src_ref=src, dst_ref=dst, send_sem=send, recv_sem=recv, device_id=device, device_id_type=MESH
        )

    def signal(sem, device):
        pl.semaphore_signal(sem, inc=1, device_id=device, device_id_type=MESH)

    def span(start, rows):
        return pl.ds(start if isinstance(start, int) else pl.multiple_of(start, 16), rows)

    def own_rows(core):
        return span((x * n_tile + core) * block_l, block_l)

    def chunk_of(owner, i):
        return span(owner * block_l + i * chunk, chunk)

    def at_r(block):
        return span(block * block_r, block_r)

    def to_x(k):
        return lax.rem(x + k + 1, n_half)

    def from_x(k):
        return lax.rem(x + n_half - k - 1, n_half)

    def greet_column(t):
        there = lax.rem(z + 1 + t, n_path)
        signal(barrier, {"path": there, "tile": lax.rem(there, n_tile)})

    loop(n_path - 1, greet_column)
    signal(barrier, {"tile": sib})
    for k in range(n_half - 1):
        signal(barrier, {"half": to_x(k), "tile": 1 - hub})

    small = [
        pltpu.make_async_copy(src, dst, small_sem.at[i])
        for i, (src, dst) in enumerate(
            ((left_map, map_l), (right_map, map_r), (branch_bits, branch_v), (cut_side, side_v))
        )
    ]
    own_left = pltpu.make_async_copy(left_prefix, left_rows.at[z], own_sem.at[0])
    own_layer = pltpu.make_async_copy(left_layer, left_w.at[own_rows(c)], own_sem.at[1])
    own_weights = pltpu.make_async_copy(right_layer, right_w, own_sem.at[2])
    own_right = pltpu.make_async_copy(right_prefix, right_rows.at[z, mine], own_sem.at[3])
    own_left.start()
    pl.when(is_hub)(own_right.start)
    for copy in small + [own_layer, own_weights]:
        copy.start()

    def prepare():
        for copy in small:
            copy.wait()
        side = spread_sides(side_v[...].astype(jnp.float32))
        branch = branch_v[...].astype(jnp.float32)
        hot_l[...] = one_hot(hot_l.shape[1], map_l[...])
        write_factor(left_factor, branch, side)
        hot_r[...] = one_hot(hot_r.shape[1], map_r[...])
        write_factor(right_factor, branch, 1.0 - side)

    def gather_out(there):
        return remote(
            right_prefix, right_rows.at[z, mine], rg_send.at[there], rg_recv.at[mine],
            {"half": there, "tile": hub},
        )

    def gather_in(owner):
        held = right_rows.at[z, owner]
        return remote(held, held, rg_send.at[0], rg_recv.at[owner], {"tile": sib})

    def weights_out(k, i):
        return remote(
            left_layer.at[pl.ds(i * chunk, chunk)], left_w.at[chunk_of(mine, i)],
            w_send.at[k, i], w_recv.at[k, i], {"half": to_x(k)},
        )

    def weights_in(k, i):
        held = left_w.at[chunk_of(from_x(k) * n_tile + c, i)]
        return remote(held, held, w_send.at[k, i], w_recv.at[k, i], {"tile": sib})

    def weights_share(k, i, core):
        held = left_w.at[chunk_of(from_x(k) * n_tile + core, i)]
        return remote(held, held, ws_send.at[k, i], ws_recv.at[k, i], {"tile": sib})

    def layer_share(core):
        return remote(left_layer, left_w.at[own_rows(core)], o_send.at[0], o_recv.at[0], {"tile": sib})

    def left_out(there):
        return remote(
            left_prefix, left_rows.at[z], lp_send.at[there], lp_recv.at[z], {"path": there}
        )

    def left_in(block):
        held = left_rows.at[block]
        return remote(held, held, lp_send.at[block], lp_recv.at[block], {"path": block})

    def blocks_out(there):
        return remote(right_rows.at[z], right_rows.at[z], rz_send.at[there], rz_recv.at[z], {"path": there})

    def blocks_in(block):
        held = right_rows.at[block]
        return remote(held, held, rz_send.at[block], rz_recv.at[block], {"path": block})

    def states_out(block):
        return remote(
            right_stage.at[block // n_tile], right_st.at[at_r(z)], st_send.at[block], st_recv.at[z], {"path": block}
        )

    def states_in(block):
        held = right_st.at[at_r(block)]
        return remote(held, held, st_send.at[block], st_recv.at[block], {"path": block})

    def states_share(block):
        held = right_st.at[at_r(block)]
        return remote(held, held, ss_send.at[block], ss_recv.at[block], {"tile": sib})

    def in_plane():
        @pl.when(jnp.logical_not(is_hub))
        def _():
            pl.semaphore_wait(barrier, n_lr - 1)
            signal(near_sem, {"tile": sib})
        @pl.when(is_hub)
        def _():
            pl.semaphore_wait(near_sem, 1)
        for k in range(n_half):
            if k == 0:
                pl.when(jnp.logical_not(is_hub))(gather_out(x).start)
            else:
                gather_out(lax.rem(x + k, n_half)).start()
        for i in range(count):
            for k in range(n_half - 1):
                weights_out(k, i).start()
        layer_share(c).start()

    def in_column():
        @pl.when(is_hub)
        def _():
            pl.semaphore_wait(barrier, (n_path - 1) * n_tile + 1)
            signal(far_sem, {"tile": sib})
        @pl.when(jnp.logical_not(is_hub))
        def _():
            pl.semaphore_wait(far_sem, 1)

    def spread(do):
        def step(t):
            d = n_path - 1 - t
            pl.when(z >= d)(lambda: do(z - d))
            pl.when(z + d < n_path)(lambda: do(z + d))
        loop(n_path - 1, step)

    def send_blocks():
        @pl.when(is_hub)
        def _():
            own_right.wait()
            others(n_lr, mine, lambda owner: gather_in(owner).wait_recv())
            spread(lambda there: blocks_out(there).start())

    def send_left():
        spread(lambda there: left_out(there).start())

    @pl.when(early)
    def _():
        in_plane()
        prepare()
        in_column()
        send_blocks()
        send_left()
    @pl.when(late)
    def _():
        in_plane()
        in_column()
        prepare()
        send_blocks()
        send_left()

    own_weights.wait()
    first = jnp.where(is_hub, z // n_tile + 1, 0)
    def form_right(j):
        block = lax.rem(first + j, per_core) * n_tile + c
        @pl.when(block != z)
        def _():
            blocks_in(block).wait_recv()
        project(proj, hot_r, right_rows[block], right_factor)
        states = nt(right_w[...], proj[...])
        @pl.when(block != z)
        def _():
            right_stage[block // n_tile] = states
            states_out(block).start()
        @pl.when(block == z)
        def _():
            right_st[at_r(z), :] = states
            states_share(z).start()

    loop(per_core, form_right)

    own_left.wait()
    others(n_path, z, lambda block: left_in(block).wait_recv())
    project(own_proj, hot_l, left_rows[...], left_factor)
    own_layer.wait()
    layer_share(sib).wait_recv()

    def pass_weights(i):
        for k in range(n_half - 1):
            weights_in(k, i).wait_recv()
            weights_share(k, i, c).start()

    def shared(i):
        for k in range(n_half - 1):
            weights_share(k, i, sib).wait_recv()

    def form_rows(t):
        @pl.when(t == 1)
        def _():
            loop(count, pass_weights)
            loop(count, shared)
        rows = span(lax.rem(x + t, n_half) * chip_l, chip_l)
        left_st[rows, :] = nt(left_w[rows, :], own_proj[...])
    loop(n_half, form_rows)

    unit = max(min(2, n_path) * block_r, 128)
    in_unit = unit // block_r
    n_units = n_path // in_unit

    def right_ready(block):
        @pl.when(is_hub)
        def _():
            @pl.when(block != z)
            def _():
                states_in(block).wait_recv()
                states_share(block).start()
        @pl.when(jnp.logical_not(is_hub))
        def _():
            states_share(block).wait_recv()

    def take_right(u):
        at = lax.rem(z // in_unit + u, n_units)
        for i in range(in_unit):
            right_ready(at * in_unit + i)
        cols = pl.ds(pl.multiple_of(at * unit, 128), unit)
        out[:, cols] = nt(left_st[...], right_st[span(at * unit, unit), :])
    others(n_path, z, lambda there: left_out(there).wait_send())
    def gather_gone(there):
        @pl.when(jnp.logical_or(there != x, jnp.logical_not(is_hub)))
        def _():
            gather_out(there).wait_send()
    loop(n_half, gather_gone)
    layer_share(c).wait_send()
    for k in range(n_half - 1):
        for i in range(count):
            weights_out(k, i).wait_send()
            weights_share(k, i, c).wait_send()
    @pl.when(is_hub)
    def _():
        others(n_path, z, lambda there: blocks_out(there).wait_send())

    loop(n_units, take_right)


    def right_gone(j):
        block = j * n_tile + c
        @pl.when(block != z)
        def _():
            states_out(block).wait_send()
    loop(per_core, right_gone)
    @pl.when(is_hub)
    def _():
        loop(n_path, lambda block: states_share(block).wait_send())


def on_device(
    sizes,
    left_prefix, right_prefix, left_layer, right_layer, left_map, right_map, branch_bits, cut_side,
):
    n_half, n_path, n_tile = sizes
    n_lr = n_half * n_tile
    paths = left_map.shape[0]
    cuts = cut_side.shape[0]
    block_l, gate = left_layer.shape
    block_r = right_layer.shape[0]
    rows_l, rows_r = block_l * n_lr, block_r * n_path
    count = block_l // chunk_rows(block_l)
    many = max(1, n_half - 1)
    dma = pltpu.SemaphoreType.DMA
    bf16, i32 = jnp.bfloat16, jnp.int32
    hbm = pl.BlockSpec(memory_space=pltpu.HBM)
    return pl.pallas_call(
        functools.partial(kernel, sizes),
        out_shape=jax.ShapeDtypeStruct((rows_l, rows_r), bf16),
        in_specs=[hbm] * 8,
        out_specs=pl.BlockSpec(memory_space=pltpu.VMEM),
        scratch_shapes=[
            pltpu.VMEM((1, paths), i32), pltpu.VMEM((1, paths), i32),
            pltpu.VMEM((cuts, paths), i32), pltpu.VMEM((1, cuts), i32),
            pltpu.VMEM((n_path,) + left_prefix.shape, bf16),
            pltpu.VMEM((n_path, n_lr) + right_prefix.shape, bf16),
            pltpu.VMEM((paths, gate), bf16), pltpu.VMEM((paths, gate), bf16),
            pltpu.VMEM((paths, gate), bf16), pltpu.VMEM((paths, gate), bf16),
            pltpu.VMEM((rows_l, gate), bf16), pltpu.VMEM((block_r, gate), bf16),
            pltpu.VMEM((rows_l, paths), bf16), pltpu.VMEM((rows_r, paths), bf16),
            pltpu.VMEM((n_path // n_tile, block_r, paths), bf16),
            pltpu.VMEM((paths, left_prefix.shape[0] * n_path), bf16),
            pltpu.VMEM((paths, right_prefix.shape[0] * n_lr), bf16),
            pltpu.SemaphoreType.REGULAR, pltpu.SemaphoreType.REGULAR, dma((4,)), dma((4,)),
            dma((1,)), dma((1,)), dma((n_path,)), dma((n_path,)),
            dma((n_half,)), dma((n_lr,)), dma((n_path,)), dma((n_path,)),
            dma((many, count)), dma((many, count)), dma((many, count)), dma((many, count)),
            dma((n_path,)), dma((n_path,)), dma((n_path,)), dma((n_path,)),
        ],
        compiler_params=pltpu.CompilerParams(
            collective_id=0, has_side_effects=True, vmem_limit_bytes=40 * 2**20
        ),
    )(*(
        pltpu.with_memory_space_constraint(array, pltpu.HBM) for array in (
            left_prefix, right_prefix, left_layer, right_layer,
            left_map[None, :], right_map[None, :], branch_bits.T, cut_side[None, :],
        )
    ))


def solution(mesh):
    in_specs = (
        P(("groups", "path"), ("half", "tile")),
        P(("groups", "half", "tile"), "path"),
        P(("groups", "half", "tile"), None),
        P(("groups", "path"), None),
        P("groups"),
        P("groups"),
        P("groups", None),
        P("groups"),
    )
    out_specs = P(("groups", "half", "tile"), "path")
    sizes = tuple(mesh.shape[axis] for axis in ("half", "path", "tile"))
    return jax.shard_map(
        functools.partial(on_device, sizes),
        mesh=mesh, in_specs=in_specs, out_specs=out_specs, check_vma=False,
    )
```

```python
import functools

import jax
import jax.numpy as jnp
from jax import lax
from jax.experimental import pallas as pl
from jax.experimental.pallas import tpu as pltpu
from jax.sharding import PartitionSpec as P

MESH = pl.DeviceIdType.MESH
NT = (((1,), (1,)), ((), ()))
TN = (((0,), (0,)), ((), ()))
FULL_MISS = 64.0
CHUNKS = 2


def chunk_rows(block):
    return max(16, block // CHUNKS // 16 * 16)


def spread_sides(side_row):
    cuts = side_row.shape[1]
    across = lax.broadcasted_iota(jnp.int32, (cuts, cuts), 0)
    down = lax.broadcasted_iota(jnp.int32, (cuts, cuts), 1)
    return jnp.sum(jnp.where(across == down, side_row, 0.0), axis=1, keepdims=True)


def write_factor(dst, branch, projector):
    cuts, gate = branch.shape[0], dst.shape[1]
    chosen = branch * projector
    table = jnp.concatenate(
        [FULL_MISS * chosen, FULL_MISS * (projector - chosen) + (branch - chosen)], axis=0
    ).astype(jnp.bfloat16)
    width = min(256, gate)
    for at in range(0, gate, width):
        place = lax.broadcasted_iota(jnp.int32, (cuts, width), 0)
        code = lax.broadcasted_iota(jnp.int32, (cuts, width), 1) + at
        bits = (jnp.right_shift(code, place) & 1).astype(jnp.float32)
        both = jnp.concatenate([1.0 - bits, bits], axis=0).astype(jnp.bfloat16)
        count = lax.dot_general(
            table, both, TN, preferred_element_type=jnp.float32
        ).astype(jnp.int32)
        sign = (1 - 2 * (count & 1)).astype(jnp.float32)
        dst[:, at:at + width] = jnp.where(count < int(FULL_MISS), sign, 0.0).astype(jnp.bfloat16)


def one_hot(rows, path_map):
    which = lax.broadcasted_iota(jnp.int32, (rows, path_map.shape[1]), 0)
    return jnp.where(which == path_map, 1.0, 0.0).T.astype(jnp.bfloat16)


def project(dst, hot, prefix, factor):
    gate = prefix.shape[-1]
    rows = prefix.astype(jnp.float32).reshape(-1, gate).astype(jnp.bfloat16)
    picks = hot[...]
    width = min(256, gate)
    for at in range(0, gate, width):
        chosen = jnp.dot(picks, rows[:, at:at + width], preferred_element_type=jnp.float32)
        dst[:, at:at + width] = chosen.astype(jnp.bfloat16) * factor[:, at:at + width]


def nt(a, b):
    return lax.dot_general(a, b, NT, preferred_element_type=jnp.float32).astype(jnp.bfloat16)


def kernel(
    sizes,
    left_prefix, right_prefix, left_layer, right_layer, left_map, right_map, branch_bits, cut_side,
    out,
    map_l, map_r, branch_v, side_v,
    left_rows, right_rows, left_factor, right_factor, own_proj, proj, left_w, right_w,
    left_st, right_st, right_stage, hot_l, hot_r,
    near_sem, far_sem, small_sem, own_sem,
    o_send, o_recv, lp_send, lp_recv, rg_send, rg_recv, rz_send, rz_recv,
    w_send, w_recv, ws_send, ws_recv, st_send, st_recv, ss_send, ss_recv,
):
    n_half, n_path, n_tile = sizes
    x, z, c = lax.axis_index("half"), lax.axis_index("path"), lax.axis_index("tile")
    sib = 1 - c
    n_lr = n_half * n_tile
    mine = x * n_tile + c
    block_l, gate = left_layer.shape
    block_r = right_layer.shape[0]
    chunk = chunk_rows(block_l)
    count = block_l // chunk
    chip_l = n_tile * block_l
    hub = lax.rem(z, n_tile)
    is_hub = c == hub
    per_core = n_path // n_tile
    early = z * 2 < n_path
    late = jnp.logical_not(early)

    barrier = pltpu.get_barrier_semaphore()

    def loop(n, do):
        if n == 1:
            do(0)
        elif n > 1:
            lax.fori_loop(0, n, lambda t, _: (do(t), 0)[1], 0)

    def others(n, me, do):
        def step(t):
            pl.when(t != me)(lambda: do(t))
        loop(n, step)

    def remote(src, dst, send, recv, device):
        return pltpu.make_async_remote_copy(
            src_ref=src, dst_ref=dst, send_sem=send, recv_sem=recv, device_id=device, device_id_type=MESH
        )

    def signal(sem, device):
        pl.semaphore_signal(sem, inc=1, device_id=device, device_id_type=MESH)

    def span(start, rows):
        return pl.ds(start if isinstance(start, int) else pl.multiple_of(start, 16), rows)

    def own_rows(core):
        return span((x * n_tile + core) * block_l, block_l)

    def chunk_of(owner, i):
        return span(owner * block_l + i * chunk, chunk)

    def at_r(block):
        return span(block * block_r, block_r)

    def to_x(k):
        return lax.rem(x + k + 1, n_half)

    def from_x(k):
        return lax.rem(x + n_half - k - 1, n_half)

    def greet_column(t):
        there = lax.rem(z + 1 + t, n_path)
        signal(barrier, {"path": there, "tile": lax.rem(there, n_tile)})

    loop(n_path - 1, greet_column)
    signal(barrier, {"tile": sib})
    for k in range(n_half - 1):
        signal(barrier, {"half": to_x(k), "tile": 1 - hub})

    small = [
        pltpu.make_async_copy(src, dst, small_sem.at[i])
        for i, (src, dst) in enumerate(
            ((left_map, map_l), (right_map, map_r), (branch_bits, branch_v), (cut_side, side_v))
        )
    ]
    own_left = pltpu.make_async_copy(left_prefix, left_rows.at[z], own_sem.at[0])
    own_layer = pltpu.make_async_copy(left_layer, left_w.at[own_rows(c)], own_sem.at[1])
    own_weights = pltpu.make_async_copy(right_layer, right_w, own_sem.at[2])
    own_right = pltpu.make_async_copy(right_prefix, right_rows.at[z, mine], own_sem.at[3])
    own_left.start()
    pl.when(is_hub)(own_right.start)
    for copy in small + [own_layer, own_weights]:
        copy.start()

    def prepare():
        for copy in small:
            copy.wait()
        side = spread_sides(side_v[...].astype(jnp.float32))
        branch = branch_v[...].astype(jnp.float32)
        hot_l[...] = one_hot(hot_l.shape[1], map_l[...])
        write_factor(left_factor, branch, side)
        hot_r[...] = one_hot(hot_r.shape[1], map_r[...])
        write_factor(right_factor, branch, 1.0 - side)

    def gather_out(there):
        return remote(
            right_prefix, right_rows.at[z, mine], rg_send.at[there], rg_recv.at[mine],
            {"half": there, "tile": hub},
        )

    def gather_in(owner):
        held = right_rows.at[z, owner]
        return remote(held, held, rg_send.at[0], rg_recv.at[owner], {"tile": sib})

    def weights_out(k, i):
        return remote(
            left_layer.at[pl.ds(i * chunk, chunk)], left_w.at[chunk_of(mine, i)],
            w_send.at[k, i], w_recv.at[k, i], {"half": to_x(k)},
        )

    def weights_in(k, i):
        held = left_w.at[chunk_of(from_x(k) * n_tile + c, i)]
        return remote(held, held, w_send.at[k, i], w_recv.at[k, i], {"tile": sib})

    def weights_share(k, i, core):
        held = left_w.at[chunk_of(from_x(k) * n_tile + core, i)]
        return remote(held, held, ws_send.at[k, i], ws_recv.at[k, i], {"tile": sib})

    def layer_share(core):
        return remote(left_layer, left_w.at[own_rows(core)], o_send.at[0], o_recv.at[0], {"tile": sib})

    def left_out(there):
        return remote(
            left_prefix, left_rows.at[z], lp_send.at[there], lp_recv.at[z], {"path": there}
        )

    def left_in(block):
        held = left_rows.at[block]
        return remote(held, held, lp_send.at[block], lp_recv.at[block], {"path": block})

    def blocks_out(there):
        return remote(right_rows.at[z], right_rows.at[z], rz_send.at[there], rz_recv.at[z], {"path": there})

    def blocks_in(block):
        held = right_rows.at[block]
        return remote(held, held, rz_send.at[block], rz_recv.at[block], {"path": block})

    def states_out(block):
        return remote(
            right_stage.at[block // n_tile], right_st.at[at_r(z)], st_send.at[block], st_recv.at[z], {"path": block}
        )

    def states_in(block):
        held = right_st.at[at_r(block)]
        return remote(held, held, st_send.at[block], st_recv.at[block], {"path": block})

    def states_share(block):
        held = right_st.at[at_r(block)]
        return remote(held, held, ss_send.at[block], ss_recv.at[block], {"tile": sib})

    def in_plane():
        @pl.when(jnp.logical_not(is_hub))
        def _():
            pl.semaphore_wait(barrier, n_lr - 1)
            signal(near_sem, {"tile": sib})
        @pl.when(is_hub)
        def _():
            pl.semaphore_wait(near_sem, 1)
        for k in range(n_half):
            if k == 0:
                pl.when(jnp.logical_not(is_hub))(gather_out(x).start)
            else:
                gather_out(lax.rem(x + k, n_half)).start()
        for i in range(count):
            for k in range(n_half - 1):
                weights_out(k, i).start()
        layer_share(c).start()

    def in_column():
        @pl.when(is_hub)
        def _():
            pl.semaphore_wait(barrier, (n_path - 1) * n_tile + 1)
            signal(far_sem, {"tile": sib})
        @pl.when(jnp.logical_not(is_hub))
        def _():
            pl.semaphore_wait(far_sem, 1)

    def spread(do):
        def step(t):
            d = n_path - 1 - t
            pl.when(z >= d)(lambda: do(z - d))
            pl.when(z + d < n_path)(lambda: do(z + d))
        loop(n_path - 1, step)

    def send_blocks():
        @pl.when(is_hub)
        def _():
            own_right.wait()
            others(n_lr, mine, lambda owner: gather_in(owner).wait_recv())
            spread(lambda there: blocks_out(there).start())

    def send_left():
        spread(lambda there: left_out(there).start())

    @pl.when(early)
    def _():
        in_plane()
        prepare()
        in_column()
        send_blocks()
        send_left()
    @pl.when(late)
    def _():
        in_plane()
        in_column()
        prepare()
        send_blocks()
        send_left()

    own_weights.wait()
    first = jnp.where(is_hub, z // n_tile + 1, 0)
    def form_right(j):
        block = lax.rem(first + j, per_core) * n_tile + c
        @pl.when(block != z)
        def _():
            blocks_in(block).wait_recv()
        project(proj, hot_r, right_rows[block], right_factor)
        states = nt(right_w[...], proj[...])
        @pl.when(block != z)
        def _():
            right_stage[block // n_tile] = states
            states_out(block).start()
        @pl.when(block == z)
        def _():
            right_st[at_r(z), :] = states
            states_share(z).start()

    loop(per_core, form_right)

    own_left.wait()
    others(n_path, z, lambda block: left_in(block).wait_recv())
    project(own_proj, hot_l, left_rows[...], left_factor)
    own_layer.wait()
    layer_share(sib).wait_recv()

    def pass_weights(i):
        for k in range(n_half - 1):
            weights_in(k, i).wait_recv()
            weights_share(k, i, c).start()

    def shared(i):
        for k in range(n_half - 1):
            weights_share(k, i, sib).wait_recv()

    def form_rows(t):
        @pl.when(t == 1)
        def _():
            loop(count, pass_weights)
            loop(count, shared)
        rows = span(lax.rem(x + t, n_half) * chip_l, chip_l)
        left_st[rows, :] = nt(left_w[rows, :], own_proj[...])
    loop(n_half, form_rows)

    unit = max(min(2, n_path) * block_r, 128)
    in_unit = unit // block_r
    n_units = n_path // in_unit

    def right_ready(block):
        @pl.when(is_hub)
        def _():
            @pl.when(block != z)
            def _():
                states_in(block).wait_recv()
                states_share(block).start()
        @pl.when(jnp.logical_not(is_hub))
        def _():
            states_share(block).wait_recv()

    def take_right(u):
        at = lax.rem(z // in_unit + u, n_units)
        for i in range(in_unit):
            right_ready(at * in_unit + i)
        cols = pl.ds(pl.multiple_of(at * unit, 128), unit)
        out[:, cols] = nt(left_st[...], right_st[span(at * unit, unit), :])
    others(n_path, z, lambda there: left_out(there).wait_send())
    def gather_gone(there):
        @pl.when(jnp.logical_or(there != x, jnp.logical_not(is_hub)))
        def _():
            gather_out(there).wait_send()
    loop(n_half, gather_gone)
    layer_share(c).wait_send()
    for k in range(n_half - 1):
        for i in range(count):
            weights_out(k, i).wait_send()
            weights_share(k, i, c).wait_send()
    @pl.when(is_hub)
    def _():
        others(n_path, z, lambda there: blocks_out(there).wait_send())

    loop(n_units, take_right)


    def right_gone(j):
        block = j * n_tile + c
        @pl.when(block != z)
        def _():
            states_out(block).wait_send()
    loop(per_core, right_gone)
    @pl.when(is_hub)
    def _():
        loop(n_path, lambda block: states_share(block).wait_send())


def on_device(
    sizes,
    left_prefix, right_prefix, left_layer, right_layer, left_map, right_map, branch_bits, cut_side,
):
    n_half, n_path, n_tile = sizes
    n_lr = n_half * n_tile
    paths = left_map.shape[0]
    cuts = cut_side.shape[0]
    block_l, gate = left_layer.shape
    block_r = right_layer.shape[0]
    rows_l, rows_r = block_l * n_lr, block_r * n_path
    count = block_l // chunk_rows(block_l)
    many = max(1, n_half - 1)
    dma = pltpu.SemaphoreType.DMA
    bf16, i32 = jnp.bfloat16, jnp.int32
    hbm = pl.BlockSpec(memory_space=pltpu.HBM)
    return pl.pallas_call(
        functools.partial(kernel, sizes),
        out_shape=jax.ShapeDtypeStruct((rows_l, rows_r), bf16),
        in_specs=[hbm] * 8,
        out_specs=pl.BlockSpec(memory_space=pltpu.VMEM),
        scratch_shapes=[
            pltpu.VMEM((1, paths), i32), pltpu.VMEM((1, paths), i32),
            pltpu.VMEM((cuts, paths), i32), pltpu.VMEM((1, cuts), i32),
            pltpu.VMEM((n_path,) + left_prefix.shape, bf16),
            pltpu.VMEM((n_path, n_lr) + right_prefix.shape, bf16),
            pltpu.VMEM((paths, gate), bf16), pltpu.VMEM((paths, gate), bf16),
            pltpu.VMEM((paths, gate), bf16), pltpu.VMEM((paths, gate), bf16),
            pltpu.VMEM((rows_l, gate), bf16), pltpu.VMEM((block_r, gate), bf16),
            pltpu.VMEM((rows_l, paths), bf16), pltpu.VMEM((rows_r, paths), bf16),
            pltpu.VMEM((n_path // n_tile, block_r, paths), bf16),
            pltpu.VMEM((paths, left_prefix.shape[0] * n_path), bf16),
            pltpu.VMEM((paths, right_prefix.shape[0] * n_lr), bf16),
            pltpu.SemaphoreType.REGULAR, pltpu.SemaphoreType.REGULAR, dma((4,)), dma((4,)),
            dma((1,)), dma((1,)), dma((n_path,)), dma((n_path,)),
            dma((n_half,)), dma((n_lr,)), dma((n_path,)), dma((n_path,)),
            dma((many, count)), dma((many, count)), dma((many, count)), dma((many, count)),
            dma((n_path,)), dma((n_path,)), dma((n_path,)), dma((n_path,)),
        ],
        compiler_params=pltpu.CompilerParams(
            collective_id=0, has_side_effects=True, vmem_limit_bytes=40 * 2**20
        ),
    )(*(
        pltpu.with_memory_space_constraint(array, pltpu.HBM) for array in (
            left_prefix, right_prefix, left_layer, right_layer,
            left_map[None, :], right_map[None, :], branch_bits.T, cut_side[None, :],
        )
    ))


def solution(mesh):
    in_specs = (
        P(("groups", "path"), ("half", "tile")),
        P(("groups", "half", "tile"), "path"),
        P(("groups", "half", "tile"), None),
        P(("groups", "path"), None),
        P("groups"),
        P("groups"),
        P("groups", None),
        P("groups"),
    )
    out_specs = P(("groups", "half", "tile"), "path")
    sizes = tuple(mesh.shape[axis] for axis in ("half", "path", "tile"))
    return jax.shard_map(
        functools.partial(on_device, sizes),
        mesh=mesh, in_specs=in_specs, out_specs=out_specs, check_vma=False,
    )
```
